32 devices in a mesh: dp: 4 (over z), expert: 8 (over y, x, core).
Axes of the slice: x: 2, y: 2, z: 4, core: 2. Of those that a mesh axis runs over, the one named last changes fastest.
Arguments:
- tokens: bfloat16 [8192, 1280], P(('dp', 'expert')), may hold values from -14 to 14
- ln_gain: float32 [1280], replicated, may hold values from 0.25 to 1.75
- router: bfloat16 [1280, 8], replicated, may hold values from -0.3125 to 0.3125
- w_in: bfloat16 [8, 5120, 1280], P('expert', 'dp'), may hold values from -0.15625 to 0.15625
- b_in: bfloat16 [8, 5120], P('expert', 'dp'), may hold values from -3 to 3
- w_out: bfloat16 [8, 5120, 1280], P('expert', 'dp'), may hold values from -0.078125 to 0.078125
- b_out: bfloat16 [8, 1280], P('expert'), may hold values from -3 to 3
- expert_choice: int32 [8192], P(('dp', 'expert')), may hold values from 0 to 7
- modality: int32 [8192], P(('dp', 'expert')), may hold values from 0 to 1, as said below
- slot: int32 [8192], P(('dp', 'expert')), may hold values from -1 to 15, as said below
Outputs:
- moe_out: bfloat16 [8192, 1280], P(('dp', 'expert'))
- aux_losses: float32 [2, 2], replicated
The draws below stay inside these ranges and needn't reach their ends.
Inputs may be any that keep to these rules, and one draw needn't show every extreme that they name: Each source's tokens with one expert and a slot other than -1 have distinct slots, numbered from 0 in token order; one expert has all 16 slots filled in every source. `modality`: every source holds tokens of both modalities.
All inputs are finite; a program needn't handle non-finite values.
Results may differ from the reference program's by a relative error of at most 0.007.
Values may be sent and summed in bfloat16 or wider, within the bound.
No kernel may reach another device: no remote copies, remote signals or barrier semaphores. Data moves between devices by JAX's collectives and lax.ppermute only.
A program may use at most 128 MiB of HBM per device.

```python
import jax
import jax.numpy as jnp
from jax import lax

D = 1280
FF = 5120
TOK_DEV = 256
EXPERTS = 8
CAP = 16
TOKENS = 8192


def routing(key):
    base = jax.random.fold_in(key, 7)
    keys = jax.random.split(base, 5)
    blocks = TOKENS // TOK_DEV
    order = jax.random.permutation(keys[0], EXPERTS)
    first = jax.random.randint(keys[1], (blocks, TOK_DEV), 0, EXPERTS)
    second = jax.random.randint(keys[2], (blocks, TOK_DEV), 0, EXPERTS)
    lowest = jnp.minimum(first, second)
    position = jax.vmap(lambda k: jax.random.permutation(k, TOK_DEV))(jax.random.split(keys[3], blocks))
    lowest = jnp.where(position < CAP, 0, lowest)
    chosen = order[lowest].astype(jnp.int32)
    table = (chosen[:, :, None] == jnp.arange(EXPERTS, dtype=jnp.int32)[None, None, :]).astype(jnp.int32)
    before = jnp.cumsum(table, axis=1) - table
    rank = jnp.sum(before * table, axis=-1)
    slots = jnp.where(rank < CAP, rank, -1).astype(jnp.int32)
    kinds = (jax.random.randint(keys[4], (blocks, TOK_DEV), 0, 4) == 0).astype(jnp.int32)
    kinds = jnp.where(position == CAP, 1, kinds)
    kinds = jnp.where(position == CAP + 1, 0, kinds).astype(jnp.int32)
    return (chosen.reshape(TOKENS), kinds.reshape(TOKENS), slots.reshape(TOKENS))


def draw_expert_choice(key, part):
    return routing(key)[0]


def draw_modality(key, part):
    return routing(key)[1]


def draw_slot(key, part):
    return routing(key)[2]


def draw_tokens(key, part):
    blocks = TOKENS // TOK_DEV
    kinds = routing(key)[1].reshape(blocks, TOK_DEV)
    keys = jax.random.split(jax.random.fold_in(key, 11), 2)
    noise = jax.random.normal(keys[0], (blocks, TOK_DEV, D), jnp.float32)
    highest = 3.0
    directions = jnp.clip(jax.random.normal(keys[1], (2, D), jnp.float32), -2.5, 2.5)
    level = highest * jnp.arange(blocks, dtype=jnp.float32) / max(blocks - 1, 1)
    chosen = jnp.where(kinds[:, :, None] == 1, directions[1][None, None, :], directions[0][None, None, :])
    values = jnp.clip(noise, -6.0, 6.0) + level[:, None, None] * chosen
    return jnp.clip(values, -14.0, 14.0).reshape(TOKENS, D).astype(jnp.bfloat16)


def block_scale(rng, shape, cuts, least, high):
    def one(axis_at, shards_of):
        heights = jax.random.uniform(jax.random.fold_in(jax.random.fold_in(rng, 6), axis_at), (shards_of,), jnp.float32, least / len(cuts), high / len(cuts))
        return jnp.repeat(jnp.exp(heights), shape[axis_at] // shards_of).reshape((-1,) + (1,) * (len(shape) - axis_at - 1))

    gain = one(*cuts[0])
    for cut in cuts[1:]:
        gain = gain * one(*cut)
    return gain


def normal_values(rng, shape, deviation, bound, cuts=(), kind=jnp.bfloat16):
    level = block_scale(rng, shape, cuts, -0.22, 0.18) if cuts else 1.0
    drawn = jax.random.normal(rng, shape, jnp.float32) * deviation * level
    return jnp.minimum(jnp.maximum(drawn, -bound), bound).astype(kind)


def setup_inputs(seed: int = 0) -> dict:
    seeds = jax.random.split(jax.random.key(seed), 11)
    tokens = draw_tokens(jax.random.fold_in(seeds[10], 71), 0)
    ln_gain = jnp.clip(1.0 + 0.15 * jax.random.normal(seeds[1], (D,), jnp.float32), 0.25, 1.75)
    router = normal_values(seeds[2], (D, EXPERTS), (D // 4) ** -0.5, 0.3125)
    w_in = normal_values(seeds[3], (EXPERTS, FF, D), D ** -0.5, 0.15625, ((0, 8), (1, 4)))
    b_in = normal_values(seeds[4], (EXPERTS, FF), 0.5, 3.0, ((0, 8), (1, 4)))
    w_out = normal_values(seeds[5], (EXPERTS, FF, D), FF ** -0.5, 0.078125, ((0, 8), (1, 4)))
    b_out = normal_values(seeds[6], (EXPERTS, D), 0.5, 3.0, ((0, 8),))
    expert_choice = draw_expert_choice(jax.random.fold_in(seeds[10], 71), 0)
    modality = draw_modality(jax.random.fold_in(seeds[10], 71), 0)
    slot = draw_slot(jax.random.fold_in(seeds[10], 71), 0)
    return dict(tokens=tokens, ln_gain=ln_gain, router=router, w_in=w_in, b_in=b_in, w_out=w_out, b_out=b_out, expert_choice=expert_choice, modality=modality, slot=slot)


def layer_norm(tokens, ln_gain):
    values = tokens.astype(jnp.float32)
    center = values - lax.optimization_barrier(jnp.mean(values, axis=-1, keepdims=True))
    spread = lax.optimization_barrier(jnp.mean(center * center, axis=-1, keepdims=True))
    return (center * lax.rsqrt(spread + 1e-06) * ln_gain).astype(jnp.bfloat16)

def reference(tokens, ln_gain, router, w_in, b_in, w_out, b_out, expert_choice, modality, slot):
    normed = layer_norm(tokens, ln_gain)
    logits = jnp.dot(normed, router, preferred_element_type=jnp.float32)
    logp = jax.nn.log_softmax(logits, axis=-1)
    probs = jnp.exp(logp)
    gate = jnp.take_along_axis(probs, expert_choice[:, None].astype(jnp.int32), axis=1)[:, 0]
    blocks = TOKENS // TOK_DEV
    source = (jnp.arange(TOKENS, dtype=jnp.int32) // TOK_DEV).astype(jnp.int32)
    place = jnp.where(slot >= 0, slot, CAP).astype(jnp.int32)
    buffer = jnp.zeros((blocks, EXPERTS, CAP + 1, D), jnp.bfloat16)
    buffer = buffer.at[source, expert_choice, place].set(normed)[:, :, :CAP]
    per_expert = jnp.transpose(buffer, (1, 0, 2, 3)).reshape(EXPERTS, blocks * CAP, D)

    def run_expert(items):
        rows, first, first_bias, second, second_bias = items
        pre = lax.dot_general(rows, first, (((1,), (1,)), ((), ())), preferred_element_type=jnp.float32)
        hidden = jax.nn.gelu(pre + first_bias.astype(jnp.float32), approximate=False).astype(jnp.bfloat16)
        result = jnp.dot(hidden, second, preferred_element_type=jnp.float32) + second_bias.astype(jnp.float32)
        return result.astype(jnp.bfloat16)
    outputs = lax.map(run_expert, (per_expert, w_in, b_in, w_out, b_out)).reshape(EXPERTS, blocks, CAP, D)
    fetched = outputs[expert_choice, source, jnp.minimum(place, CAP - 1)]
    kept = (slot >= 0)[:, None]
    moe_out = jnp.where(kept, gate[:, None] * fetched.astype(jnp.float32), 0.0).astype(jnp.bfloat16)
    textual = (modality == 1).astype(jnp.float32)
    select = jnp.stack([1.0 - textual, textual], axis=0)
    entropy = -lax.optimization_barrier(jnp.sum(probs * logp, axis=-1))
    prob_sum = jnp.dot(select, probs, precision=lax.Precision.HIGHEST)
    ent_sum = jnp.dot(select, entropy, precision=lax.Precision.HIGHEST)
    count = lax.optimization_barrier(jnp.sum(select, axis=1))
    pbar = prob_sum / count[:, None]
    aux_losses = jnp.stack([ent_sum / count, lax.optimization_barrier(jnp.sum(pbar * jnp.log(pbar), axis=1))], axis=1)
    return (moe_out, aux_losses)
```

```python
import functools

import jax
import jax.numpy as jnp
from jax import lax
from jax.experimental import pallas as pl
from jax.experimental.pallas import tpu as pltpu
from jax.sharding import PartitionSpec as P

CAP = 16
CHUNKS = 2
AXES = ("dp", "expert")
VMEM = pl.BlockSpec(memory_space=pltpu.VMEM)


def dispatch_kernel(copies, chunk, tokens, gain, target, normed_out, *buffers):
    values = tokens[...].astype(jnp.float32)
    center = values - jnp.mean(values, axis=-1, keepdims=True)
    spread = jnp.mean(center * center, axis=-1, keepdims=True)
    normed = (center * lax.rsqrt(spread + 1e-06) * gain[...]).astype(jnp.bfloat16)
    normed_out[...] = normed
    for index, buffer in enumerate(buffers):
        rows = buffer.shape[1]
        row = lax.broadcasted_iota(jnp.int32, (rows, normed.shape[0]), 0)
        key = (row // chunk) * CAP + index * chunk + row % chunk
        table = (key == target[...]).astype(jnp.float32).astype(jnp.bfloat16)
        packed = jnp.dot(table, normed, preferred_element_type=jnp.float32).astype(jnp.bfloat16)
        for copy in range(copies):
            buffer[copy] = packed


def router_kernel(normed, router, choice, modality, gate_out, stats_out):
    logits = lax.dot_general(
        router[...], normed[...], (((1,), (1,)), ((), ())), preferred_element_type=jnp.float32
    )
    peak = jnp.max(logits, axis=0, keepdims=True)
    shifted = logits - peak
    logp = shifted - jnp.log(jnp.sum(jnp.exp(shifted), axis=0, keepdims=True))
    probs = jnp.exp(logp)
    expert = lax.broadcasted_iota(jnp.int32, probs.shape, 0)
    gate = jnp.sum(jnp.where(expert == choice[...], probs, 0.0), axis=0, keepdims=True)
    gate_out[...] = jnp.broadcast_to(gate, gate_out.shape)
    textual = (modality[...] == 1).astype(jnp.float32)
    entropy = -jnp.sum(probs * logp, axis=0, keepdims=True)
    lane = lax.broadcasted_iota(jnp.int32, stats_out.shape, 1)
    stats = jnp.zeros(stats_out.shape, jnp.float32)
    for kind, select in enumerate((1.0 - textual, textual)):
        prob_sum = jnp.sum(probs * select, axis=1, keepdims=True)
        ent_sum = jnp.sum(entropy * select, axis=1, keepdims=True)
        count = jnp.sum(select, axis=1, keepdims=True)
        for place, value in enumerate((prob_sum, ent_sum, count)):
            stats = jnp.where(lane == 2 * place + kind, value, stats)
    stats_out[...] = stats


def expert_kernel(rows, first, first_bias, second, last_bias, out, total):
    step = pl.program_id(0)

    @pl.when(step == 0)
    def _():
        total[...] = jnp.broadcast_to(last_bias[...], total.shape)

    pre = lax.dot_general(
        rows[...], first[...], (((1,), (1,)), ((), ())), preferred_element_type=jnp.float32
    )
    pre = pre + first_bias[...].astype(jnp.float32)
    hidden = (0.5 * pre * (1.0 + lax.erf(pre * (0.5**0.5)))).astype(jnp.bfloat16)
    total[...] += jnp.dot(hidden, second[...], preferred_element_type=jnp.float32)

    @pl.when(step == pl.num_programs(0) - 1)
    def _():
        out[...] = total[...].astype(jnp.bfloat16)


def combine_kernel(chunk, target, gate, stats, *refs):
    returned, (out, aux) = refs[:-2], refs[-2:]
    fetched = None
    experts = stats.shape[1]
    for index, part in enumerate(returned):
        row = lax.broadcasted_iota(jnp.int32, (part.shape[0], target.shape[1]), 0)
        row = row % (experts * chunk)
        key = (row // chunk) * CAP + index * chunk + row % chunk
        table = (key == target[...]).astype(jnp.float32).astype(jnp.bfloat16)
        term = lax.dot_general(
            table, part[...], (((0,), (0,)), ((), ())), preferred_element_type=jnp.float32
        )
        fetched = term if fetched is None else fetched + term
    scale = jnp.transpose(gate[...])[:, 0:1]
    out[...] = (scale * fetched).astype(jnp.bfloat16)
    sums = jnp.sum(stats[...], axis=0)
    row = lax.broadcasted_iota(jnp.int32, aux.shape, 0)
    column = lax.broadcasted_iota(jnp.int32, aux.shape, 1)
    result = jnp.zeros(aux.shape, jnp.float32)
    for kind in range(2):
        count = sums[0:1, 4 + kind : 5 + kind]
        local = sums[0:1, 2 + kind : 3 + kind] / count
        pbar = sums[:, kind : kind + 1] / sums[:, 4 + kind : 5 + kind]
        spread = jnp.sum(pbar * jnp.log(pbar), axis=0, keepdims=True)
        result = jnp.where((row == kind) & (column == 0), local, result)
        result = jnp.where((row == kind) & (column == 1), spread, result)
    aux[...] = result


def on_device(tokens, ln_gain, router, w_in, b_in, w_out, b_out, expert_choice, modality, slot):
    count, width = tokens.shape
    experts = router.shape[1]
    layers, senders = lax.axis_size("dp"), lax.axis_size("expert")
    assert w_in.shape[0] == 1 and experts == senders
    chunk = CAP // CHUNKS
    target = jnp.where(slot >= 0, expert_choice * CAP + slot, -1).reshape(1, count)
    normed, *buffers = pl.pallas_call(
        functools.partial(dispatch_kernel, layers, chunk),
        out_shape=[jax.ShapeDtypeStruct((count, width), jnp.bfloat16)]
        + [jax.ShapeDtypeStruct((layers, experts * chunk, width), jnp.bfloat16)] * CHUNKS,
        in_specs=[VMEM] * 3,
        out_specs=[VMEM] * (1 + CHUNKS),
        name="dispatch",
    )(tokens, ln_gain.reshape(1, width), target)
    devices = layers * senders

    def exchange(block):
        return lax.all_to_all(
            block.reshape(devices, chunk, width), AXES, split_axis=0, concat_axis=0, tiled=True
        ).reshape(devices * chunk, width)

    received = [exchange(buffer) for buffer in buffers]
    gate, stats = pl.pallas_call(
        router_kernel,
        out_shape=[
            jax.ShapeDtypeStruct((8, count), jnp.float32),
            jax.ShapeDtypeStruct((experts, 128), jnp.float32),
        ],
        in_specs=[VMEM] * 4,
        out_specs=[VMEM] * 2,
        name="router",
    )(normed, router.T, expert_choice.reshape(1, count), modality.reshape(1, count))
    stats = lax.all_to_all(
        jnp.broadcast_to(stats[None], (devices, experts, 128)), AXES, split_axis=0, concat_axis=0, tiled=True
    )
    hidden = w_in.shape[1]
    block = 256
    rows = devices * chunk
    last_bias = jnp.where(lax.axis_index("dp") == 0, b_out.astype(jnp.float32), 0.0)
    returned = []
    for part in received:
        partial = pl.pallas_call(
            expert_kernel,
            grid=(hidden // block,),
            out_shape=jax.ShapeDtypeStruct((rows, width), jnp.bfloat16),
            in_specs=[
                pl.BlockSpec((rows, width), lambda i: (0, 0)),
                pl.BlockSpec((None, block, width), lambda i: (0, i, 0)),
                pl.BlockSpec((1, block), lambda i: (0, i)),
                pl.BlockSpec((None, block, width), lambda i: (0, i, 0)),
                pl.BlockSpec((1, width), lambda i: (0, 0)),
            ],
            out_specs=pl.BlockSpec((rows, width), lambda i: (0, 0)),
            scratch_shapes=[pltpu.VMEM((rows, width), jnp.float32)],
            cost_estimate=pl.CostEstimate(
                flops=4 * rows * width * hidden,
                bytes_accessed=4 * width * (hidden + rows),
                transcendentals=rows * hidden,
            ),
            name="expert",
        )(part, w_in, b_in, w_out, last_bias)
        returned.append(exchange(partial))
    return pl.pallas_call(
        functools.partial(combine_kernel, chunk),
        out_shape=[
            jax.ShapeDtypeStruct((count, width), jnp.bfloat16),
            jax.ShapeDtypeStruct((2, 2), jnp.float32),
        ],
        in_specs=[VMEM] * (3 + CHUNKS),
        out_specs=[VMEM] * 2,
        name="combine",
    )(target, gate, stats, *returned)


def solution(mesh):
    return jax.shard_map(
        on_device,
        mesh=mesh,
        in_specs=(
            P(AXES, None),
            P(),
            P(),
            P("expert", "dp", None),
            P("expert", "dp"),
            P("expert", "dp", None),
            P("expert", None),
            P(AXES),
            P(AXES),
            P(AXES),
        ),
        out_specs=(P(AXES, None), P()),
        check_vma=False,
    )
```

```python
import functools

import jax
import jax.numpy as jnp
from jax import lax
from jax.experimental import pallas as pl
from jax.experimental.pallas import tpu as pltpu
from jax.sharding import PartitionSpec as P

CAP = 16
CHUNKS = 2
LANES = 128
AXES = ("dp", "expert")
VMEM = pl.BlockSpec(memory_space=pltpu.VMEM)


def role(layer):
    return (layer ^ (layer >> 1)) & 1


def one_hot(chunk, index, experts, rows, target):
    row = lax.broadcasted_iota(jnp.int32, (rows, target.shape[1]), 0)
    row = row % (experts * chunk)
    key = (row // chunk) * CAP + index * chunk + row % chunk
    return (key == target).astype(jnp.float32).astype(jnp.bfloat16)


def dispatch_kernel(copies, chunk, experts, tokens, gain, choice, slot, normed_out, target_out, *buffers):
    values = tokens[...].astype(jnp.float32)
    center = values - jnp.mean(values, axis=-1, keepdims=True)
    spread = jnp.mean(center * center, axis=-1, keepdims=True)
    normed = (center * lax.rsqrt(spread + 1e-06) * gain[...]).astype(jnp.bfloat16)
    normed_out[...] = normed
    target = jnp.where(slot[...] >= 0, choice[...] * CAP + slot[...], -1)
    target_out[...] = target
    for index, buffer in enumerate(buffers):
        table = one_hot(chunk, index, experts, experts * chunk, target)
        packed = jnp.dot(table, normed, preferred_element_type=jnp.float32).astype(jnp.bfloat16)
        for copy in range(copies):
            buffer[copy] = packed


def router_kernel(normed, router, choice, modality, gate_out, stats_out):
    logits = lax.dot_general(
        router[...], normed[...], (((1,), (1,)), ((), ())), preferred_element_type=jnp.float32
    )
    shifted = logits - jnp.max(logits, axis=0, keepdims=True)
    logp = shifted - jnp.log(jnp.sum(jnp.exp(shifted), axis=0, keepdims=True))
    probs = jnp.exp(logp)
    experts = probs.shape[0]
    expert = lax.broadcasted_iota(jnp.int32, probs.shape, 0)
    gate = jnp.sum(jnp.where(expert == choice[...], probs, 0.0), axis=0, keepdims=True)
    gate_out[...] = jnp.broadcast_to(gate, gate_out.shape)
    textual = (modality[...] == 1).astype(jnp.float32)
    entropy = -jnp.sum(probs * logp, axis=0, keepdims=True)
    lane = lax.broadcasted_iota(jnp.int32, (experts, LANES), 1)
    row = lax.broadcasted_iota(jnp.int32, (experts, LANES), 0)
    line = lane[0:1]
    stats = jnp.zeros((1, LANES), jnp.float32)
    for kind, select in enumerate((1.0 - textual, textual)):
        prob_sum = jnp.sum(probs * select, axis=1, keepdims=True)
        spread = jnp.where(lane == row + kind * experts, prob_sum, 0.0)
        stats = stats + jnp.sum(spread, axis=0, keepdims=True)
        ent_sum = jnp.sum(entropy * select, axis=1, keepdims=True)
        count = jnp.sum(select, axis=1, keepdims=True)
        stats = jnp.where(line == 2 * experts + kind, ent_sum, stats)
        stats = jnp.where(line == 2 * experts + 2 + kind, count, stats)
    stats_out[...] = jnp.broadcast_to(stats, stats_out.shape)


def expert_kernel(rows, first, first_bias, second, last_bias, out):
    pre = lax.dot_general(
        rows[...], first[...], (((1,), (1,)), ((), ())), preferred_element_type=jnp.float32
    )
    pre = pre + first_bias[...].astype(jnp.float32)
    hidden = (0.5 * pre * (1.0 + lax.erf(pre * (0.5**0.5)))).astype(jnp.bfloat16)
    result = jnp.dot(hidden, second[...], preferred_element_type=jnp.float32)
    out[...] = (result + last_bias[...]).astype(out.dtype)


def sum_kernel(chunk, carry, own, other, stats, other_stats, out):
    width = own.shape[1]
    out[:, :width] = (own[...] + other[...].astype(jnp.float32)).astype(jnp.bfloat16)
    if carry:
        total = stats[0:1] + other_stats[0:1]
        row = lax.broadcasted_iota(jnp.int32, (own.shape[0], LANES), 0) % chunk
        extra = jnp.zeros(row.shape, jnp.float32)
        for piece in range(3):
            part = total.astype(jnp.bfloat16).astype(jnp.float32)
            extra = jnp.where(row == piece, part, extra)
            total = total - part
        out[:, width:] = extra.astype(jnp.bfloat16)


def combine_kernel(chunk, experts, target, gate, *refs):
    returned, (out, aux) = refs[:-2], refs[-2:]
    width = out.shape[1]
    fetched = None
    for index, part in enumerate(returned):
        table = one_hot(chunk, index, experts, part.shape[0], target[...])
        term = lax.dot_general(
            table, part[:, :width], (((0,), (0,)), ((), ())), preferred_element_type=jnp.float32
        )
        fetched = term if fetched is None else fetched + term
    scale = jnp.transpose(gate[...])[:, 0:1]
    out[...] = (scale * fetched).astype(jnp.bfloat16)
    sums = jnp.sum(returned[-1][:, width:].astype(jnp.float32), axis=0, keepdims=True)
    lane = lax.broadcasted_iota(jnp.int32, sums.shape, 1)

    def pick(at):
        return jnp.sum(jnp.where(lane == at, sums, 0.0), axis=1, keepdims=True)

    row = lax.broadcasted_iota(jnp.int32, aux.shape, 0)
    column = lax.broadcasted_iota(jnp.int32, aux.shape, 1)
    result = jnp.zeros(aux.shape, jnp.float32)
    for kind in range(2):
        count = pick(2 * experts + 2 + kind)
        local = pick(2 * experts + kind) / count
        pbar = sums / count
        inside = (lane >= kind * experts) & (lane < (kind + 1) * experts)
        terms = jnp.where(inside, pbar * jnp.log(pbar), 0.0)
        spread = jnp.sum(terms, axis=1, keepdims=True)
        result = jnp.where((row == kind) & (column == 0), local, result)
        result = jnp.where((row == kind) & (column == 1), spread, result)
    aux[...] = result


def on_device(tokens, ln_gain, router, w_in, b_in, w_out, b_out, expert_choice, modality, slot):
    count, width = tokens.shape
    experts = router.shape[1]
    layers, senders = lax.axis_size("dp"), lax.axis_size("expert")
    assert w_in.shape[0] == 1 and experts == senders and layers % 4 == 0
    assert 2 * experts + 4 <= LANES
    hidden = w_in.shape[1]
    chunk = CAP // CHUNKS
    half = layers // 2
    peers = half * experts
    rows = peers * chunk
    groups = [
        [z * experts + e for z in range(layers) if role(z) == r for e in range(experts)] for r in range(2)
    ]
    pairs = [(z, z ^ 1) for z in range(layers)]
    choice = expert_choice.reshape(1, count)
    normed, target, *buffers = pl.pallas_call(
        functools.partial(dispatch_kernel, half, chunk, experts),
        out_shape=[
            jax.ShapeDtypeStruct((count, width), jnp.bfloat16),
            jax.ShapeDtypeStruct((1, count), jnp.int32),
        ]
        + [jax.ShapeDtypeStruct((half, experts * chunk, width), jnp.bfloat16)] * CHUNKS,
        in_specs=[VMEM] * 4,
        out_specs=[VMEM] * (2 + CHUNKS),
        name="dispatch",
    )(tokens, ln_gain.reshape(1, width), choice, slot.reshape(1, count))

    def exchange(block):
        return lax.all_to_all(
            block.reshape(peers, chunk, block.shape[-1]),
            AXES,
            split_axis=0,
            concat_axis=0,
            axis_index_groups=groups,
            tiled=True,
        ).reshape(rows, block.shape[-1])

    def swap(block):
        return lax.ppermute(block, "dp", pairs)

    gate, stats = pl.pallas_call(
        router_kernel,
        out_shape=[
            jax.ShapeDtypeStruct((8, count), jnp.float32),
            jax.ShapeDtypeStruct((8, LANES), jnp.float32),
        ],
        in_specs=[VMEM] * 4,
        out_specs=[VMEM] * 2,
        name="router",
    )(normed, router.T, choice, modality.reshape(1, count))
    other_stats = swap(stats)

    height = rows if rows <= 512 else 256

    def run_expert(part, bias, dtype, name):
        return pl.pallas_call(
            expert_kernel,
            grid=(rows // height,),
            out_shape=jax.ShapeDtypeStruct((rows, width), dtype),
            in_specs=[
                pl.BlockSpec((height, width), lambda i: (i, 0)),
                pl.BlockSpec((None, hidden, width), lambda i: (0, 0, 0)),
                pl.BlockSpec((1, hidden), lambda i: (0, 0)),
                pl.BlockSpec((None, hidden, width), lambda i: (0, 0, 0)),
                pl.BlockSpec((1, width), lambda i: (0, 0)),
            ],
            out_specs=pl.BlockSpec((height, width), lambda i: (i, 0)),
            cost_estimate=pl.CostEstimate(
                flops=4 * rows * width * hidden,
                bytes_accessed=4 * width * (hidden + rows),
                transcendentals=rows * hidden,
            ),
            name=name,
        )(part, w_in, b_in, w_out, bias)

    last_bias = jnp.where(lax.axis_index("dp") < 2, b_out.astype(jnp.float32), 0.0)
    no_bias = jnp.zeros((1, width), jnp.float32)
    returned = []
    for index, buffer in enumerate(buffers):
        carry = index == CHUNKS - 1
        mine = exchange(buffer)
        theirs = swap(mine)
        own = run_expert(mine, last_bias, jnp.float32, "own")
        back = swap(run_expert(theirs, no_bias, jnp.bfloat16, "theirs"))
        full = width + LANES if carry else width
        summed = pl.pallas_call(
            functools.partial(sum_kernel, chunk, carry),
            grid=(rows // height,),
            out_shape=jax.ShapeDtypeStruct((rows, full), jnp.bfloat16),
            in_specs=[pl.BlockSpec((height, width), lambda i: (i, 0))] * 2
            + [pl.BlockSpec((8, LANES), lambda i: (0, 0))] * 2,
            out_specs=pl.BlockSpec((height, full), lambda i: (i, 0)),
            name="sum",
        )(own, back, stats, other_stats)
        returned.append(exchange(summed))
    return pl.pallas_call(
        functools.partial(combine_kernel, chunk, experts),
        out_shape=[
            jax.ShapeDtypeStruct((count, width), jnp.bfloat16),
            jax.ShapeDtypeStruct((2, 2), jnp.float32),
        ],
        in_specs=[VMEM] * (2 + CHUNKS),
        out_specs=[VMEM] * 2,
        name="combine",
    )(target, gate, *returned)


def solution(mesh):
    return jax.shard_map(
        on_device,
        mesh=mesh,
        in_specs=(
            P(AXES, None),
            P(),
            P(),
            P("expert", "dp", None),
            P("expert", "dp"),
            P("expert", "dp", None),
            P("expert", None),
            P(AXES),
            P(AXES),
            P(AXES),
        ),
        out_specs=(P(AXES, None), P()),
        check_vma=False,
    )
```

```python
import functools

import jax
import jax.numpy as jnp
from jax import lax
from jax.experimental import pallas as pl
from jax.experimental.pallas import tpu as pltpu
from jax.sharding import PartitionSpec as P

CAP = 16
CHUNKS = 1
SPLIT = 2
LANES = 128
AXES = ("dp", "expert")
VMEM = pl.BlockSpec(memory_space=pltpu.VMEM)
PARAMS = pltpu.CompilerParams(vmem_limit_bytes=24 << 20)


def role(layer):
    return (layer ^ (layer >> 1)) & 1


def one_hot(chunk, index, experts, rows, target):
    row = lax.broadcasted_iota(jnp.int32, (rows, target.shape[1]), 0)
    row = row % (experts * chunk)
    key = (row // chunk) * CAP + index * chunk + row % chunk
    return (key == target).astype(jnp.float32).astype(jnp.bfloat16)


def dispatch_kernel(copies, chunk, experts, tokens, gain, choice, slot, normed_out, target_out, *buffers):
    values = tokens[...].astype(jnp.float32)
    center = values - jnp.mean(values, axis=-1, keepdims=True)
    spread = jnp.mean(center * center, axis=-1, keepdims=True)
    normed = (center * lax.rsqrt(spread + 1e-06) * gain[...].reshape(1, values.shape[1])).astype(jnp.bfloat16)
    normed_out[...] = normed
    target = jnp.where(slot[...] >= 0, choice[...] * CAP + slot[...], -1)
    target_out[...] = target
    for index, buffer in enumerate(buffers):
        table = one_hot(chunk, index, experts, experts * chunk, target)
        packed = jnp.dot(table, normed, preferred_element_type=jnp.float32).astype(jnp.bfloat16)
        for copy in range(copies):
            buffer[copy] = packed


def router_kernel(normed, router, choice, modality, gate_out, stats_out):
    logits = lax.dot_general(
        router[...], normed[...], (((1,), (1,)), ((), ())), preferred_element_type=jnp.float32
    )
    shifted = logits - jnp.max(logits, axis=0, keepdims=True)
    logp = shifted - jnp.log(jnp.sum(jnp.exp(shifted), axis=0, keepdims=True))
    probs = jnp.exp(logp)
    experts = probs.shape[0]
    expert = lax.broadcasted_iota(jnp.int32, probs.shape, 0)
    gate = jnp.sum(jnp.where(expert == choice[...], probs, 0.0), axis=0, keepdims=True)
    gate_out[...] = jnp.broadcast_to(gate, gate_out.shape)
    textual = (modality[...] == 1).astype(jnp.float32)
    entropy = -jnp.sum(probs * logp, axis=0, keepdims=True)
    lane = lax.broadcasted_iota(jnp.int32, (experts, LANES), 1)
    row = lax.broadcasted_iota(jnp.int32, (experts, LANES), 0)
    line = lane[0:1]
    stats = jnp.zeros((1, LANES), jnp.float32)
    for kind, select in enumerate((1.0 - textual, textual)):
        prob_sum = jnp.sum(probs * select, axis=1, keepdims=True)
        spread = jnp.where(lane == row + kind * experts, prob_sum, 0.0)
        stats = stats + jnp.sum(spread, axis=0, keepdims=True)
        ent_sum = jnp.sum(entropy * select, axis=1, keepdims=True)
        count = jnp.sum(select, axis=1, keepdims=True)
        stats = jnp.where(line == 2 * experts + kind, ent_sum, stats)
        stats = jnp.where(line == 2 * experts + 2 + kind, count, stats)
    stats_out[...] = jnp.broadcast_to(stats, stats_out.shape)


def expert_kernel(biased, rows, first, first_bias, second, last_bias, out):
    pre = lax.dot_general(
        rows[...], first[...], (((1,), (1,)), ((), ())), preferred_element_type=jnp.float32
    )
    pre = pre + first_bias[...].astype(jnp.float32)
    hidden = (0.5 * pre * (1.0 + lax.erf(pre * (0.5**0.5)))).astype(jnp.bfloat16)
    result = jnp.dot(hidden, second[...], preferred_element_type=jnp.float32)
    if biased:
        once = (lax.axis_index("dp") < 2).astype(jnp.float32)
        result = result + once * last_bias[...].astype(jnp.float32)
    out[...] = result.astype(out.dtype)


def sum_kernel(chunk, carry, steps, own, *refs):
    others, (stats, other_stats, out) = refs[:-3], refs[-3:]
    width = own.shape[1]
    part = pl.program_id(0) // steps
    other = others[0][...]
    for index in range(1, len(others)):
        other = jnp.where(part == index, others[index][...], other)
    out[:, :width] = (own[...] + other.astype(jnp.float32)).astype(jnp.bfloat16)
    if carry:
        total = stats[0:1] + other_stats[0:1]
        row = lax.broadcasted_iota(jnp.int32, (own.shape[0], LANES), 0) % chunk
        extra = jnp.zeros(row.shape, jnp.float32)
        for piece in range(3):
            rounded = total.astype(jnp.bfloat16).astype(jnp.float32)
            extra = jnp.where(row == piece, rounded, extra)
            total = total - rounded
        out[:, width:] = extra.astype(jnp.bfloat16)


def combine_kernel(chunk, experts, target, gate, *refs):
    returned, (out, aux) = refs[:-2], refs[-2:]
    width = out.shape[1]
    fetched = None
    for index, part in enumerate(returned):
        table = one_hot(chunk, index, experts, part.shape[0], target[...])
        term = lax.dot_general(
            table, part[:, :width], (((0,), (0,)), ((), ())), preferred_element_type=jnp.float32
        )
        fetched = term if fetched is None else fetched + term
    scale = jnp.transpose(gate[...])[:, 0:1]
    out[...] = (scale * fetched).astype(jnp.bfloat16)
    sums = jnp.sum(returned[-1][:, width:].astype(jnp.float32), axis=0, keepdims=True)
    lane = lax.broadcasted_iota(jnp.int32, sums.shape, 1)

    def pick(at):
        return jnp.sum(jnp.where(lane == at, sums, 0.0), axis=1, keepdims=True)

    row = lax.broadcasted_iota(jnp.int32, aux.shape, 0)
    column = lax.broadcasted_iota(jnp.int32, aux.shape, 1)
    result = jnp.zeros(aux.shape, jnp.float32)
    for kind in range(2):
        count = pick(2 * experts + 2 + kind)
        local = pick(2 * experts + kind) / count
        pbar = sums / count
        inside = (lane >= kind * experts) & (lane < (kind + 1) * experts)
        terms = jnp.where(inside, pbar * jnp.log(pbar), 0.0)
        spread = jnp.sum(terms, axis=1, keepdims=True)
        result = jnp.where((row == kind) & (column == 0), local, result)
        result = jnp.where((row == kind) & (column == 1), spread, result)
    aux[...] = result


def on_device(tokens, ln_gain, router, w_in, b_in, w_out, b_out, expert_choice, modality, slot):
    count, width = tokens.shape
    experts = router.shape[1]
    layers, senders = lax.axis_size("dp"), lax.axis_size("expert")
    assert w_in.shape[0] == 1 and experts == senders and layers % 4 == 0
    assert 2 * experts + 4 <= LANES
    hidden = w_in.shape[1]
    chunk = CAP // CHUNKS
    half = layers // 2
    peers = half * experts
    rows = peers * chunk
    groups = [
        [z * experts + e for z in range(layers) if role(z) == r for e in range(experts)] for r in range(2)
    ]
    pairs = [(z, z ^ 1) for z in range(layers)]
    choice = expert_choice.reshape(1, count)
    normed, target, *buffers = pl.pallas_call(
        functools.partial(dispatch_kernel, half, chunk, experts),
        out_shape=[
            jax.ShapeDtypeStruct((count, width), jnp.bfloat16),
            jax.ShapeDtypeStruct((1, count), jnp.int32),
        ]
        + [jax.ShapeDtypeStruct((half, experts * chunk, width), jnp.bfloat16)] * CHUNKS,
        in_specs=[VMEM] * 4,
        out_specs=[VMEM] * (2 + CHUNKS),
        name="dispatch",
    )(tokens, ln_gain, choice, slot.reshape(1, count))

    def exchange(block):
        return lax.all_to_all(
            block.reshape(peers, chunk, block.shape[-1]),
            AXES,
            split_axis=0,
            concat_axis=0,
            axis_index_groups=groups,
            tiled=True,
        ).reshape(rows, block.shape[-1])

    def swap(block):
        return lax.ppermute(block, "dp", pairs)

    gate, stats = pl.pallas_call(
        router_kernel,
        out_shape=[
            jax.ShapeDtypeStruct((8, count), jnp.float32),
            jax.ShapeDtypeStruct((8, LANES), jnp.float32),
        ],
        in_specs=[VMEM] * 4,
        out_specs=[VMEM] * 2,
        compiler_params=PARAMS,
        name="router",
    )(normed, router.T, choice, modality.reshape(1, count))
    other_stats = swap(stats)

    first = pltpu.with_memory_space_constraint(w_in.reshape(hidden, width), pltpu.VMEM)
    second = pltpu.with_memory_space_constraint(w_out.reshape(hidden, width), pltpu.VMEM)

    def run_expert(part, biased, dtype, name):
        tall = part.shape[0]
        height = min(tall, 256)
        return pl.pallas_call(
            functools.partial(expert_kernel, biased),
            grid=(tall // height,),
            out_shape=jax.ShapeDtypeStruct((tall, width), dtype),
            in_specs=[
                pl.BlockSpec((height, width), lambda i: (i, 0)),
                VMEM,
                pl.BlockSpec((1, hidden), lambda i: (0, 0)),
                VMEM,
                pl.BlockSpec((1, width), lambda i: (0, 0)),
            ],
            out_specs=pl.BlockSpec((height, width), lambda i: (i, 0)),
            cost_estimate=pl.CostEstimate(
                flops=4 * tall * width * hidden,
                bytes_accessed=4 * width * (hidden + tall),
                transcendentals=tall * hidden,
            ),
            compiler_params=PARAMS,
            name=name,
        )(part, first, b_in, second, b_out)

    returned = []
    for index, buffer in enumerate(buffers):
        carry = index == CHUNKS - 1
        mine = exchange(buffer)
        tall = rows // SPLIT
        theirs = [swap(mine[at : at + tall]) for at in range(0, rows, tall)]
        own = run_expert(mine, True, jnp.float32, "own")
        back = [swap(run_expert(part, False, jnp.bfloat16, "theirs")) for part in theirs]
        full = width + LANES if carry else width
        height = min(tall, 256)
        steps = tall // height
        summed = pl.pallas_call(
            functools.partial(sum_kernel, chunk, carry, steps),
            grid=(rows // height,),
            out_shape=jax.ShapeDtypeStruct((rows, full), jnp.bfloat16),
            in_specs=[pl.BlockSpec((height, width), lambda i: (i, 0))]
            + [
                pl.BlockSpec((height, width), lambda i, p=p: (jnp.clip(i - p * steps, 0, steps - 1), 0))
                for p in range(SPLIT)
            ]
            + [pl.BlockSpec((8, LANES), lambda i: (0, 0))] * 2,
            out_specs=pl.BlockSpec((height, full), lambda i: (i, 0)),
            compiler_params=PARAMS,
            name="sum",
        )(own, *back, stats, other_stats)
        returned.append(exchange(summed))
    return pl.pallas_call(
        functools.partial(combine_kernel, chunk, experts),
        out_shape=[
            jax.ShapeDtypeStruct((count, width), jnp.bfloat16),
            jax.ShapeDtypeStruct((2, 2), jnp.float32),
        ],
        in_specs=[VMEM] * (2 + CHUNKS),
        out_specs=[VMEM] * 2,
        compiler_params=PARAMS,
        name="combine",
    )(target, gate, *returned)


def solution(mesh):
    return jax.shard_map(
        on_device,
        mesh=mesh,
        in_specs=(
            P(AXES, None),
            P(),
            P(),
            P("expert", "dp", None),
            P("expert", "dp"),
            P("expert", "dp", None),
            P("expert", None),
            P(AXES),
            P(AXES),
            P(AXES),
        ),
        out_specs=(P(AXES, None), P()),
        check_vma=False,
    )
```

```python
import functools

import jax
import jax.numpy as jnp
from jax import lax
from jax.experimental import pallas as pl
from jax.experimental.pallas import tpu as pltpu
from jax.sharding import PartitionSpec as P

CAP = 16
PARTS = 2
LANES = 128
AXES = ("dp", "expert")
VMEM = pl.BlockSpec(memory_space=pltpu.VMEM)
PARAMS = pltpu.CompilerParams(vmem_limit_bytes=24 << 20)


def one_hot(rows, target):
    row = lax.broadcasted_iota(jnp.int32, (rows, target.shape[1]), 0)
    return (row == target).astype(jnp.float32).astype(jnp.bfloat16)


def spread_stats(total, rows, period):
    row = lax.broadcasted_iota(jnp.int32, (rows, LANES), 0) % period
    out = jnp.zeros((rows, LANES), jnp.float32)
    for piece in range(3):
        rounded = total.astype(jnp.bfloat16).astype(jnp.float32)
        out = jnp.where(row == piece, rounded, out)
        total = total - rounded
    return out.astype(jnp.bfloat16)


def join_stats(block):
    return jnp.sum(block.astype(jnp.float32), axis=0, keepdims=True)


def dispatch_kernel(tokens, gain, choice, slot, normed_out, target_out, buffer):
    values = tokens[...].astype(jnp.float32)
    center = values - jnp.mean(values, axis=-1, keepdims=True)
    spread = jnp.mean(center * center, axis=-1, keepdims=True)
    scaled = center * lax.rsqrt(spread + 1e-06) * gain[...].reshape(1, values.shape[1])
    normed = scaled.astype(jnp.bfloat16)
    normed_out[...] = normed
    target = jnp.where(slot[...] >= 0, choice[...] * CAP + slot[...], -1)
    target_out[...] = target
    table = one_hot(buffer.shape[0], target)
    buffer[...] = jnp.dot(table, normed, preferred_element_type=jnp.float32).astype(jnp.bfloat16)


def router_kernel(normed, router, choice, modality, first, second, gate_out, stats_out):
    logits = lax.dot_general(
        router[...], normed[...], (((1,), (1,)), ((), ())), preferred_element_type=jnp.float32
    )
    shifted = logits - jnp.max(logits, axis=0, keepdims=True)
    logp = shifted - jnp.log(jnp.sum(jnp.exp(shifted), axis=0, keepdims=True))
    probs = jnp.exp(logp)
    experts = probs.shape[0]
    expert = lax.broadcasted_iota(jnp.int32, probs.shape, 0)
    gate = jnp.sum(jnp.where(expert == choice[...], probs, 0.0), axis=0, keepdims=True)
    gate_out[...] = jnp.broadcast_to(gate, gate_out.shape)
    textual = (modality[...] == 1).astype(jnp.float32)
    entropy = -jnp.sum(probs * logp, axis=0, keepdims=True)
    lane = lax.broadcasted_iota(jnp.int32, (experts, LANES), 1)
    row = lax.broadcasted_iota(jnp.int32, (experts, LANES), 0)
    line = lane[0:1]
    stats = jnp.zeros((1, LANES), jnp.float32)
    for kind, select in enumerate((1.0 - textual, textual)):
        prob_sum = jnp.sum(probs * select, axis=1, keepdims=True)
        spread = jnp.where(lane == row + kind * experts, prob_sum, 0.0)
        stats = stats + jnp.sum(spread, axis=0, keepdims=True)
        ent_sum = jnp.sum(entropy * select, axis=1, keepdims=True)
        count = jnp.sum(select, axis=1, keepdims=True)
        stats = jnp.where(line == 2 * experts + kind, ent_sum, stats)
        stats = jnp.where(line == 2 * experts + 2 + kind, count, stats)
    stats_out[...] = jnp.broadcast_to(stats, stats_out.shape)


def expert_kernel(carry, rows, first, first_bias, second, *refs):
    stats, out = refs if carry else (None, refs[0])
    pre = lax.dot_general(
        rows[...], first[...], (((1,), (1,)), ((), ())), preferred_element_type=jnp.float32
    )
    pre = pre + first_bias[...].astype(jnp.float32)
    hidden = (0.5 * pre * (1.0 + lax.erf(pre * (0.5**0.5)))).astype(jnp.bfloat16)
    result = jnp.dot(hidden, second[...], preferred_element_type=jnp.float32)
    if carry:
        width = result.shape[1]
        out[:, :width] = result.astype(out.dtype)
        out[:, width:] = spread_stats(stats[0:1], out.shape[0], out.shape[0])
    else:
        out[...] = result.astype(out.dtype)


def far_kernel(carry, own, other, *refs):
    out = refs[-1]
    width = own.shape[1]
    out[:, :width] = (own[...] + other[:, :width].astype(jnp.float32)).astype(jnp.bfloat16)
    if carry:
        stats, other_stats = refs[0], refs[1]
        total = stats[0:1] + join_stats(other_stats[:, width:])
        out[:, width:] = spread_stats(total, out.shape[0], out.shape[0])


def near_kernel(parts, own, other, bias, stats, other_stats, *refs):
    far, out = refs[:-1], refs[-1]
    width = own.shape[1]
    result = own[...] + other[...].astype(jnp.float32) + bias[...].astype(jnp.float32)
    total = stats[0:1] + join_stats(other_stats[:, width:])
    tall = own.shape[0] // parts
    for part in range(parts):
        rows = slice(part * tall, (part + 1) * tall)
        piece = result[rows]
        for block in far[part::parts]:
            piece = piece + block[:, :width].astype(jnp.float32)
        out[rows, :width] = piece.astype(jnp.bfloat16)
    for block in far[::parts]:
        total = total + join_stats(block[:, width:])
    out[:, width:] = spread_stats(total, out.shape[0], CAP)


def combine_kernel(experts, target, gate, returned, out, aux):
    width = out.shape[1]
    table = one_hot(returned.shape[0], target[...])
    fetched = lax.dot_general(
        table, returned[:, :width], (((0,), (0,)), ((), ())), preferred_element_type=jnp.float32
    )
    scale = jnp.transpose(gate[...])[:, 0:1]
    out[...] = (scale * fetched).astype(jnp.bfloat16)
    sums = join_stats(returned[:, width:])
    lane = lax.broadcasted_iota(jnp.int32, sums.shape, 1)

    def pick(at):
        return jnp.sum(jnp.where(lane == at, sums, 0.0), axis=1, keepdims=True)

    row = lax.broadcasted_iota(jnp.int32, aux.shape, 0)
    column = lax.broadcasted_iota(jnp.int32, aux.shape, 1)
    result = jnp.zeros(aux.shape, jnp.float32)
    for kind in range(2):
        count = pick(2 * experts + 2 + kind)
        local = pick(2 * experts + kind) / count
        pbar = sums / count
        inside = (lane >= kind * experts) & (lane < (kind + 1) * experts)
        terms = jnp.where(inside, pbar * jnp.log(pbar), 0.0)
        spread = jnp.sum(terms, axis=1, keepdims=True)
        result = jnp.where((row == kind) & (column == 0), local, result)
        result = jnp.where((row == kind) & (column == 1), spread, result)
    aux[...] = result


def on_device(tokens, ln_gain, router, w_in, b_in, w_out, b_out, expert_choice, modality, slot):
    count, width = tokens.shape
    experts = router.shape[1]
    layers, senders = lax.axis_size("dp"), lax.axis_size("expert")
    assert w_in.shape[0] == 1 and experts == senders and layers % 4 == 0
    assert 2 * experts + 4 <= LANES
    hidden = w_in.shape[1]
    rows = experts * CAP
    tall = rows // PARTS
    full = width + LANES
    far_steps = [m ^ ((m >> 1) & 1) for m in range(2, layers, 2)]
    choice = expert_choice.reshape(1, count)
    normed, target, buffer = pl.pallas_call(
        dispatch_kernel,
        out_shape=[
            jax.ShapeDtypeStruct((count, width), jnp.bfloat16),
            jax.ShapeDtypeStruct((1, count), jnp.int32),
            jax.ShapeDtypeStruct((rows, width), jnp.bfloat16),
        ],
        in_specs=[VMEM] * 4,
        out_specs=[VMEM] * 3,
        name="dispatch",
    )(tokens, ln_gain, choice, slot.reshape(1, count))

    def exchange(block):
        return lax.all_to_all(
            block.reshape(experts, CAP, block.shape[-1]), "expert", split_axis=0, concat_axis=0, tiled=True
        ).reshape(rows, block.shape[-1])

    def swap(block, step):
        return lax.ppermute(block, "dp", [(z, z ^ step) for z in range(layers)])

    home = exchange(buffer)
    halves = [home[at : at + tall] for at in range(0, rows, tall)]
    visitors = [swap(part, step) for step in far_steps for part in halves]
    beside = swap(home, 1)
    first = pltpu.with_memory_space_constraint(w_in.reshape(hidden, width), pltpu.VMEM)
    second = pltpu.with_memory_space_constraint(w_out.reshape(hidden, width), pltpu.VMEM)
    gate, stats = pl.pallas_call(
        router_kernel,
        out_shape=[
            jax.ShapeDtypeStruct((8, count), jnp.float32),
            jax.ShapeDtypeStruct((8, LANES), jnp.float32),
        ],
        in_specs=[VMEM] * 6,
        out_specs=[VMEM] * 2,
        compiler_params=PARAMS,
        name="router",
    )(normed, router.T, choice, modality.reshape(1, count), first, second)

    def run_expert(part, dtype, carry=False):
        size = part.shape[0]
        columns = full if carry else width
        return pl.pallas_call(
            functools.partial(expert_kernel, carry),
            out_shape=jax.ShapeDtypeStruct((size, columns), dtype),
            in_specs=[VMEM] * (5 if carry else 4),
            out_specs=VMEM,
            cost_estimate=pl.CostEstimate(
                flops=4 * size * width * hidden,
                bytes_accessed=4 * width * (hidden + size),
                transcendentals=size * hidden,
            ),
            compiler_params=PARAMS,
        )(*((part, first, b_in, second) + ((stats,) if carry else ())))

    forwarded = [swap(part, 1) for part in visitors]
    answers = [
        swap(run_expert(part, jnp.bfloat16, index % PARTS == 0), 1)
        for index, part in enumerate(forwarded)
    ]
    answer = swap(run_expert(beside, jnp.bfloat16), 1)
    returned = []
    for index, part in enumerate(visitors):
        carry = index % PARTS == 0
        own = run_expert(part, jnp.float32)
        operands = (own, answers[index]) + ((stats, answers[0]) if carry else ())
        summed = pl.pallas_call(
            functools.partial(far_kernel, carry),
            out_shape=jax.ShapeDtypeStruct((tall, full if carry else width), jnp.bfloat16),
            in_specs=[VMEM] * len(operands),
            out_specs=VMEM,
            compiler_params=PARAMS,
            name="far_sum",
        )(*operands)
        returned.append(swap(summed, far_steps[index // PARTS]))
    own = run_expert(home, jnp.float32)
    summed = pl.pallas_call(
        functools.partial(near_kernel, PARTS),
        out_shape=jax.ShapeDtypeStruct((rows, full), jnp.bfloat16),
        in_specs=[VMEM] * (5 + len(returned)),
        out_specs=VMEM,
        compiler_params=PARAMS,
        name="near_sum",
    )(own, answer, b_out, stats, answers[0], *returned)
    return pl.pallas_call(
        functools.partial(combine_kernel, experts),
        out_shape=[
            jax.ShapeDtypeStruct((count, width), jnp.bfloat16),
            jax.ShapeDtypeStruct((2, 2), jnp.float32),
        ],
        in_specs=[VMEM] * 3,
        out_specs=[VMEM] * 2,
        compiler_params=PARAMS,
        name="combine",
    )(target, gate, exchange(summed))


def solution(mesh):
    return jax.shard_map(
        on_device,
        mesh=mesh,
        in_specs=(
            P(AXES, None),
            P(),
            P(),
            P("expert", "dp", None),
            P("expert", "dp"),
            P("expert", "dp", None),
            P("expert", None),
            P(AXES),
            P(AXES),
            P(AXES),
        ),
        out_specs=(P(AXES, None), P()),
        check_vma=False,
    )
```

```python
import functools

import jax
import jax.numpy as jnp
from jax import lax
from jax.experimental import pallas as pl
from jax.experimental.pallas import tpu as pltpu
from jax.sharding import PartitionSpec as P

CAP = 16
PARTS = 2
LANES = 128
AXES = ("dp", "expert")
VMEM = pl.BlockSpec(memory_space=pltpu.VMEM)
PARAMS = pltpu.CompilerParams(vmem_limit_bytes=24 << 20)


def one_hot(rows, target):
    row = lax.broadcasted_iota(jnp.int32, (rows, target.shape[1]), 0)
    return (row == target).astype(jnp.float32).astype(jnp.bfloat16)


def spread_stats(total, rows, period):
    row = lax.broadcasted_iota(jnp.int32, (rows, LANES), 0) % period
    out = jnp.zeros((rows, LANES), jnp.float32)
    for piece in range(3):
        rounded = total.astype(jnp.bfloat16).astype(jnp.float32)
        out = jnp.where(row == piece, rounded, out)
        total = total - rounded
    return out.astype(jnp.bfloat16)


def join_stats(block):
    return jnp.sum(block.astype(jnp.float32), axis=0, keepdims=True)


def dispatch_kernel(tokens, gain, choice, slot, normed_out, target_out, *slabs):
    values = tokens[...].astype(jnp.float32)
    center = values - jnp.mean(values, axis=-1, keepdims=True)
    spread = jnp.mean(center * center, axis=-1, keepdims=True)
    scaled = center * lax.rsqrt(spread + 1e-06) * gain[...].reshape(1, values.shape[1])
    normed = scaled.astype(jnp.bfloat16)
    normed_out[...] = normed
    distance = choice[...] ^ lax.axis_index("expert")
    target = jnp.where(slot[...] >= 0, distance * CAP + slot[...], -1)
    target_out[...] = target
    table = one_hot(len(slabs) * CAP, target)
    packed = jnp.dot(table, normed, preferred_element_type=jnp.float32).astype(jnp.bfloat16)
    for index, slab in enumerate(slabs):
        slab[...] = packed[index * CAP : (index + 1) * CAP]


def pack_kernel(*refs):
    slabs, out = refs[:-1], refs[-1]
    for index, slab in enumerate(slabs):
        out[index * CAP : (index + 1) * CAP] = slab[...]


def router_kernel(normed, router, choice, modality, first, second, gate_out, stats_out):
    logits = lax.dot_general(
        router[...], normed[...], (((1,), (1,)), ((), ())), preferred_element_type=jnp.float32
    )
    shifted = logits - jnp.max(logits, axis=0, keepdims=True)
    logp = shifted - jnp.log(jnp.sum(jnp.exp(shifted), axis=0, keepdims=True))
    probs = jnp.exp(logp)
    experts = probs.shape[0]
    expert = lax.broadcasted_iota(jnp.int32, probs.shape, 0)
    gate = jnp.sum(jnp.where(expert == choice[...], probs, 0.0), axis=0, keepdims=True)
    gate_out[...] = jnp.broadcast_to(gate, gate_out.shape)
    textual = (modality[...] == 1).astype(jnp.float32)
    entropy = -jnp.sum(probs * logp, axis=0, keepdims=True)
    lane = lax.broadcasted_iota(jnp.int32, (experts, LANES), 1)
    row = lax.broadcasted_iota(jnp.int32, (experts, LANES), 0)
    line = lane[0:1]
    stats = jnp.zeros((1, LANES), jnp.float32)
    for kind, select in enumerate((1.0 - textual, textual)):
        prob_sum = jnp.sum(probs * select, axis=1, keepdims=True)
        spread = jnp.where(lane == row + kind * experts, prob_sum, 0.0)
        stats = stats + jnp.sum(spread, axis=0, keepdims=True)
        ent_sum = jnp.sum(entropy * select, axis=1, keepdims=True)
        count = jnp.sum(select, axis=1, keepdims=True)
        stats = jnp.where(line == 2 * experts + kind, ent_sum, stats)
        stats = jnp.where(line == 2 * experts + 2 + kind, count, stats)
    stats_out[...] = jnp.broadcast_to(stats, stats_out.shape)


def expert_kernel(count, carry, *refs):
    parts, (first, first_bias, second), rest = refs[:count], refs[count : count + 3], refs[count + 3 :]
    out = rest[-1]
    rows = parts[0][...] if count == 1 else jnp.concatenate([part[...] for part in parts], axis=0)
    pre = lax.dot_general(
        rows, first[...], (((1,), (1,)), ((), ())), preferred_element_type=jnp.float32
    )
    pre = pre + first_bias[...].astype(jnp.float32)
    hidden = (0.5 * pre * (1.0 + lax.erf(pre * (0.5**0.5)))).astype(jnp.bfloat16)
    result = jnp.dot(hidden, second[...], preferred_element_type=jnp.float32)
    width = result.shape[1]
    out[:, :width] = result.astype(out.dtype)
    if carry:
        out[:, width:] = spread_stats(rest[0][0:1], out.shape[0], out.shape[0])


def far_kernel(index, carry, own, other, *refs):
    out = refs[-1]
    tall, width = out.shape[0], own.shape[1]
    mine = own[index * tall : (index + 1) * tall]
    out[:, :width] = (mine + other[:, :width].astype(jnp.float32)).astype(jnp.bfloat16)
    if carry:
        total = refs[0][0:1] + join_stats(refs[1][:, width:])
        out[:, width:] = spread_stats(total, tall, tall)


def near_kernel(index, far_count, own, other, bias, *refs):
    far, refs = refs[:far_count], refs[far_count:]
    tall, width = far[0].shape[0], own.shape[1]
    rows = slice(index * tall, (index + 1) * tall)
    result = own[rows] + other[rows].astype(jnp.float32) + bias[...].astype(jnp.float32)
    for block in far:
        result = result + block[:, :width].astype(jnp.float32)
    result = result.astype(jnp.bfloat16)
    if index == 0:
        stats, other_stats, extra_out = refs[:3]
        total = stats[0:1] + join_stats(other_stats[:, width:])
        for block in far:
            total = total + join_stats(block[:, width:])
        extra = spread_stats(total, CAP, CAP)
        extra_out[...] = extra
        slabs = refs[3:]
    else:
        extra = refs[0][...]
        slabs = refs[1:]
    for place, slab in enumerate(slabs):
        slab[:, :width] = result[place * CAP : (place + 1) * CAP]
        slab[:, width:] = extra


def combine_kernel(experts, target, gate, *refs):
    slabs, (out, aux) = refs[:-2], refs[-2:]
    width = out.shape[1]
    returned = jnp.concatenate([slab[...] for slab in slabs], axis=0)
    table = one_hot(returned.shape[0], target[...])
    fetched = lax.dot_general(
        table, returned[:, :width], (((0,), (0,)), ((), ())), preferred_element_type=jnp.float32
    )
    scale = jnp.transpose(gate[...])[:, 0:1]
    out[...] = (scale * fetched).astype(jnp.bfloat16)
    sums = join_stats(slabs[0][:, width:])
    have = {0: sums}
    for index in range(1, experts):
        have[index] = join_stats(slabs[index][:, width:])
    while len(have) > 1:
        have = {at // 2: have[at] + have[at + 1] for at in range(0, len(have), 2)}
    sums = have[0]
    lane = lax.broadcasted_iota(jnp.int32, sums.shape, 1)

    def pick(at):
        return jnp.sum(jnp.where(lane == at, sums, 0.0), axis=1, keepdims=True)

    row = lax.broadcasted_iota(jnp.int32, aux.shape, 0)
    column = lax.broadcasted_iota(jnp.int32, aux.shape, 1)
    result = jnp.zeros(aux.shape, jnp.float32)
    for kind in range(2):
        count = pick(2 * experts + 2 + kind)
        local = pick(2 * experts + kind) / count
        pbar = sums / count
        inside = (lane >= kind * experts) & (lane < (kind + 1) * experts)
        terms = jnp.where(inside, pbar * jnp.log(pbar), 0.0)
        spread = jnp.sum(terms, axis=1, keepdims=True)
        result = jnp.where((row == kind) & (column == 0), local, result)
        result = jnp.where((row == kind) & (column == 1), spread, result)
    aux[...] = result


def on_device(tokens, ln_gain, router, w_in, b_in, w_out, b_out, expert_choice, modality, slot):
    count, width = tokens.shape
    experts = router.shape[1]
    layers, senders = lax.axis_size("dp"), lax.axis_size("expert")
    assert w_in.shape[0] == 1 and experts == senders and layers % 4 == 0
    assert 2 * experts + 4 <= LANES
    hidden = w_in.shape[1]
    rows = experts * CAP
    tall = rows // PARTS
    full = width + LANES
    far_steps = [m ^ ((m >> 1) & 1) for m in range(2, layers, 2)]
    choice = expert_choice.reshape(1, count)
    normed, target, *slabs = pl.pallas_call(
        dispatch_kernel,
        out_shape=[
            jax.ShapeDtypeStruct((count, width), jnp.bfloat16),
            jax.ShapeDtypeStruct((1, count), jnp.int32),
        ]
        + [jax.ShapeDtypeStruct((CAP, width), jnp.bfloat16)] * experts,
        in_specs=[VMEM] * 4,
        out_specs=[VMEM] * (2 + experts),
        name="dispatch",
    )(tokens, ln_gain, choice, slot.reshape(1, count))

    def kernel(body, shapes, *operands, cost=None):
        many = isinstance(shapes, list)
        return pl.pallas_call(
            body,
            out_shape=shapes,
            in_specs=[VMEM] * len(operands),
            out_specs=[VMEM] * len(shapes) if many else VMEM,
            cost_estimate=cost,
            compiler_params=PARAMS,
        )(*operands)

    def bf16(*shape):
        return jax.ShapeDtypeStruct(shape, jnp.bfloat16)

    def f32(*shape):
        return jax.ShapeDtypeStruct(shape, jnp.float32)

    def hop(block, axis, step):
        size = lax.axis_size(axis)
        return lax.ppermute(block, axis, [(i, i ^ step) for i in range(size)])

    each = experts // PARTS
    homes, visitors, beside = [], {}, []
    slabs = [slabs[0]] + [hop(slabs[k], "expert", k) for k in range(1, experts)]
    for part in range(PARTS):
        home = kernel(pack_kernel, bf16(tall, width), *slabs[part * each : (part + 1) * each])
        homes.append(home)
        for step in far_steps:
            visitors[step, part] = hop(home, "dp", step)
        beside.append(hop(home, "dp", 1))
    first = pltpu.with_memory_space_constraint(w_in.reshape(hidden, width), pltpu.VMEM)
    second = pltpu.with_memory_space_constraint(w_out.reshape(hidden, width), pltpu.VMEM)
    gate, stats = kernel(
        router_kernel,
        [f32(8, count), f32(8, LANES)],
        normed,
        router.T,
        choice,
        modality.reshape(1, count),
        first,
        second,
    )

    def run_expert(parts, dtype, carry=False):
        size = sum(part.shape[0] for part in parts)
        return kernel(
            functools.partial(expert_kernel, len(parts), carry),
            jax.ShapeDtypeStruct((size, full if carry else width), dtype),
            *parts,
            first,
            b_in,
            second,
            *((stats,) if carry else ()),
            cost=pl.CostEstimate(
                flops=4 * size * width * hidden,
                bytes_accessed=4 * width * (hidden + size),
                transcendentals=size * hidden,
            ),
        )

    order = [(step, part) for part in range(PARTS) for step in far_steps]
    forwarded = {at: hop(visitors[at], "dp", 1) for at in order}
    answers = {}
    for at in order:
        theirs = run_expert([forwarded[at]], jnp.bfloat16, at[1] == 0)
        answers[at] = hop(theirs, "dp", 1)
    theirs = run_expert(beside, jnp.bfloat16)
    answer = hop(theirs, "dp", 1)
    owns = {}
    for step in far_steps:
        owns[step] = run_expert([visitors[step, part] for part in range(PARTS)], jnp.float32)
    returned = {}
    shared = answers[far_steps[0], 0]
    for step, part in order:
        carry = part == 0
        summed = kernel(
            functools.partial(far_kernel, part, carry),
            bf16(tall, full if carry else width),
            owns[step],
            answers[step, part],
            *((stats, shared) if carry else ()),
        )
        returned[step, part] = hop(summed, "dp", step)
    own = run_expert(homes, jnp.float32)
    back, extra = [], None
    for part in range(PARTS):
        far = [returned[step, part] for step in far_steps]
        shapes = [bf16(CAP, full)] * each
        body = functools.partial(near_kernel, part, len(far))
        if part == 0:
            out = kernel(body, [bf16(CAP, LANES)] + shapes, own, answer, b_out, *far, stats, shared)
            extra, out = out[0], out[1:]
        else:
            out = kernel(body, shapes, own, answer, b_out, *far, extra)
        for place, slab in enumerate(out):
            k = part * each + place
            back.append(hop(slab, "expert", k) if k else slab)
    return tuple(
        kernel(
            functools.partial(combine_kernel, experts),
            [bf16(count, width), f32(2, 2)],
            target,
            gate,
            *back,
        )
    )


def solution(mesh):
    return jax.shard_map(
        on_device,
        mesh=mesh,
        in_specs=(
            P(AXES, None),
            P(),
            P(),
            P("expert", "dp", None),
            P("expert", "dp"),
            P("expert", "dp", None),
            P("expert", None),
            P(AXES),
            P(AXES),
            P(AXES),
        ),
        out_specs=(P(AXES, None), P()),
        check_vma=False,
    )
```

```python
import functools

import jax
import jax.numpy as jnp
from jax import lax
from jax.experimental import pallas as pl
from jax.experimental.pallas import tpu as pltpu
from jax.sharding import PartitionSpec as P

CAP = 16
PARTS = 2
LANES = 128
AXES = ("dp", "expert")
VMEM = pl.BlockSpec(memory_space=pltpu.VMEM)
PARAMS = pltpu.CompilerParams(vmem_limit_bytes=24 << 20)


def one_hot(rows, target):
    row = lax.broadcasted_iota(jnp.int32, (rows, target.shape[1]), 0)
    return (row == target).astype(jnp.float32).astype(jnp.bfloat16)


def spread_stats(total, rows, period):
    row = lax.broadcasted_iota(jnp.int32, (rows, LANES), 0) % period
    out = jnp.zeros((rows, LANES), jnp.float32)
    for piece in range(3):
        rounded = total.astype(jnp.bfloat16).astype(jnp.float32)
        out = jnp.where(row == piece, rounded, out)
        total = total - rounded
    return out.astype(jnp.bfloat16)


def join_stats(block):
    return jnp.sum(block.astype(jnp.float32), axis=0, keepdims=True)


def dispatch_kernel(tokens, gain, choice, slot, normed_out, target_out, buffer):
    values = tokens[...].astype(jnp.float32)
    center = values - jnp.mean(values, axis=-1, keepdims=True)
    spread = jnp.mean(center * center, axis=-1, keepdims=True)
    scaled = center * lax.rsqrt(spread + 1e-06) * gain[...].reshape(1, values.shape[1])
    normed = scaled.astype(jnp.bfloat16)
    normed_out[...] = normed
    kept = slot[...] >= 0
    relative = choice[...] ^ lax.axis_index("expert")
    target_out[...] = jnp.where(kept, relative * CAP + slot[...], -1)
    table = one_hot(buffer.shape[0], jnp.where(kept, choice[...] * CAP + slot[...], -1))
    buffer[...] = jnp.dot(table, normed, preferred_element_type=jnp.float32).astype(jnp.bfloat16)


def pack_kernel(received, home, *parts):
    me = lax.axis_index("expert")
    each = parts[0].shape[0] // CAP
    for k in range(home.shape[0] // CAP):
        slab = received[pl.ds(pl.multiple_of((me ^ k) * CAP, CAP), CAP)]
        home[k * CAP : (k + 1) * CAP] = slab
        at = (k % each) * CAP
        parts[k // each][at : at + CAP] = slab


def router_kernel(normed, router, choice, modality, first, second, gate_out, stats_out):
    logits = lax.dot_general(
        router[...], normed[...], (((1,), (1,)), ((), ())), preferred_element_type=jnp.float32
    )
    shifted = logits - jnp.max(logits, axis=0, keepdims=True)
    logp = shifted - jnp.log(jnp.sum(jnp.exp(shifted), axis=0, keepdims=True))
    probs = jnp.exp(logp)
    experts = probs.shape[0]
    expert = lax.broadcasted_iota(jnp.int32, probs.shape, 0)
    gate = jnp.sum(jnp.where(expert == choice[...], probs, 0.0), axis=0, keepdims=True)
    gate_out[...] = jnp.broadcast_to(gate, gate_out.shape)
    textual = (modality[...] == 1).astype(jnp.float32)
    entropy = -jnp.sum(probs * logp, axis=0, keepdims=True)
    lane = lax.broadcasted_iota(jnp.int32, (experts, LANES), 1)
    row = lax.broadcasted_iota(jnp.int32, (experts, LANES), 0)
    line = lane[0:1]
    stats = jnp.zeros((1, LANES), jnp.float32)
    for kind, select in enumerate((1.0 - textual, textual)):
        prob_sum = jnp.sum(probs * select, axis=1, keepdims=True)
        spread = jnp.where(lane == row + kind * experts, prob_sum, 0.0)
        stats = stats + jnp.sum(spread, axis=0, keepdims=True)
        ent_sum = jnp.sum(entropy * select, axis=1, keepdims=True)
        count = jnp.sum(select, axis=1, keepdims=True)
        stats = jnp.where(line == 2 * experts + kind, ent_sum, stats)
        stats = jnp.where(line == 2 * experts + 2 + kind, count, stats)
    stats_out[...] = jnp.broadcast_to(stats, stats_out.shape)


def expert_kernel(count, carry, *refs):
    parts, (first, first_bias, second), rest = refs[:count], refs[count : count + 3], refs[count + 3 :]
    out = rest[-1]
    rows = parts[0][...] if count == 1 else jnp.concatenate([part[...] for part in parts], axis=0)
    pre = lax.dot_general(
        rows, first[...], (((1,), (1,)), ((), ())), preferred_element_type=jnp.float32
    )
    pre = pre + first_bias[...].astype(jnp.float32)
    hidden = (0.5 * pre * (1.0 + lax.erf(pre * (0.5**0.5)))).astype(jnp.bfloat16)
    result = jnp.dot(hidden, second[...], preferred_element_type=jnp.float32)
    width = result.shape[1]
    out[:, :width] = result.astype(out.dtype)
    if carry:
        out[:, width:] = spread_stats(rest[0][0:1], out.shape[0], out.shape[0])


def far_kernel(index, carry, own, other, *refs):
    out = refs[-1]
    tall, width = out.shape[0], own.shape[1]
    mine = own[index * tall : (index + 1) * tall]
    out[:, :width] = (mine + other[:, :width].astype(jnp.float32)).astype(jnp.bfloat16)
    if carry:
        total = refs[0][0:1] + join_stats(refs[1][:, width:])
        out[:, width:] = spread_stats(total, tall, tall)


def near_kernel(index, far_count, own, other, bias, *refs):
    far, refs = refs[:far_count], refs[far_count:]
    tall, width = far[0].shape[0], own.shape[1]
    rows = slice(index * tall, (index + 1) * tall)
    result = own[rows] + other[rows].astype(jnp.float32) + bias[...].astype(jnp.float32)
    for block in far:
        result = result + block[:, :width].astype(jnp.float32)
    result = result.astype(jnp.bfloat16)
    if index == 0:
        stats, other_stats, extra_out = refs[:3]
        total = stats[0:1] + join_stats(other_stats[:, width:])
        for block in far:
            total = total + join_stats(block[:, width:])
        extra = spread_stats(total, CAP, CAP)
        extra_out[...] = extra
        slabs = refs[3:]
    else:
        extra = refs[0][...]
        slabs = refs[1:]
    for place, slab in enumerate(slabs):
        slab[:, :width] = result[place * CAP : (place + 1) * CAP]
        slab[:, width:] = extra


def combine_kernel(experts, target, gate, *refs):
    slabs, (out, aux) = refs[:-2], refs[-2:]
    width = out.shape[1]
    returned = jnp.concatenate([slab[...] for slab in slabs], axis=0)
    table = one_hot(returned.shape[0], target[...])
    fetched = lax.dot_general(
        table, returned[:, :width], (((0,), (0,)), ((), ())), preferred_element_type=jnp.float32
    )
    scale = jnp.transpose(gate[...])[:, 0:1]
    out[...] = (scale * fetched).astype(jnp.bfloat16)
    sums = join_stats(slabs[0][:, width:])
    have = {0: sums}
    for index in range(1, experts):
        have[index] = join_stats(slabs[index][:, width:])
    while len(have) > 1:
        have = {at // 2: have[at] + have[at + 1] for at in range(0, len(have), 2)}
    sums = have[0]
    lane = lax.broadcasted_iota(jnp.int32, sums.shape, 1)

    def pick(at):
        return jnp.sum(jnp.where(lane == at, sums, 0.0), axis=1, keepdims=True)

    row = lax.broadcasted_iota(jnp.int32, aux.shape, 0)
    column = lax.broadcasted_iota(jnp.int32, aux.shape, 1)
    result = jnp.zeros(aux.shape, jnp.float32)
    for kind in range(2):
        count = pick(2 * experts + 2 + kind)
        local = pick(2 * experts + kind) / count
        pbar = sums / count
        inside = (lane >= kind * experts) & (lane < (kind + 1) * experts)
        terms = jnp.where(inside, pbar * jnp.log(pbar), 0.0)
        spread = jnp.sum(terms, axis=1, keepdims=True)
        result = jnp.where((row == kind) & (column == 0), local, result)
        result = jnp.where((row == kind) & (column == 1), spread, result)
    aux[...] = result


def on_device(tokens, ln_gain, router, w_in, b_in, w_out, b_out, expert_choice, modality, slot):
    count, width = tokens.shape
    experts = router.shape[1]
    layers, senders = lax.axis_size("dp"), lax.axis_size("expert")
    assert w_in.shape[0] == 1 and experts == senders and layers % 4 == 0
    assert 2 * experts + 4 <= LANES and experts & (experts - 1) == 0
    hidden = w_in.shape[1]
    rows = experts * CAP
    tall = rows // PARTS
    full = width + LANES
    far_steps = [m ^ ((m >> 1) & 1) for m in range(2, layers, 2)]
    choice = expert_choice.reshape(1, count)
    normed, target, buffer = pl.pallas_call(
        dispatch_kernel,
        out_shape=[
            jax.ShapeDtypeStruct((count, width), jnp.bfloat16),
            jax.ShapeDtypeStruct((1, count), jnp.int32),
            jax.ShapeDtypeStruct((rows, width), jnp.bfloat16),
        ],
        in_specs=[VMEM] * 4,
        out_specs=[VMEM] * 3,
        name="dispatch",
    )(tokens, ln_gain, choice, slot.reshape(1, count))

    def kernel(body, shapes, *operands, cost=None):
        many = isinstance(shapes, list)
        return pl.pallas_call(
            body,
            out_shape=shapes,
            in_specs=[VMEM] * len(operands),
            out_specs=[VMEM] * len(shapes) if many else VMEM,
            cost_estimate=cost,
            compiler_params=PARAMS,
            name="kernel",
        )(*operands)

    def bf16(*shape):
        return jax.ShapeDtypeStruct(shape, jnp.bfloat16)

    def f32(*shape):
        return jax.ShapeDtypeStruct(shape, jnp.float32)

    def hop(block, axis, step):
        size = lax.axis_size(axis)
        return lax.ppermute(block, axis, [(i, i ^ step) for i in range(size)])

    each = experts // PARTS
    received = lax.all_to_all(
        buffer.reshape(experts, CAP, width), "expert", split_axis=0, concat_axis=0, tiled=True
    ).reshape(rows, width)
    home, *homes = kernel(pack_kernel, [bf16(rows, width)] + [bf16(tall, width)] * PARTS, received)
    beside = hop(home, "dp", 1)
    visitors = {
        (step, part): hop(homes[part], "dp", step)
        for part in range(PARTS)
        for step in far_steps
    }
    first = pltpu.with_memory_space_constraint(w_in.reshape(hidden, width), pltpu.VMEM)
    second = pltpu.with_memory_space_constraint(w_out.reshape(hidden, width), pltpu.VMEM)
    gate, stats = kernel(
        router_kernel,
        [f32(8, count), f32(8, LANES)],
        normed,
        router.T,
        choice,
        modality.reshape(1, count),
        first,
        second,
    )

    def run_expert(parts, dtype, carry=False):
        size = sum(part.shape[0] for part in parts)
        return kernel(
            functools.partial(expert_kernel, len(parts), carry),
            jax.ShapeDtypeStruct((size, full if carry else width), dtype),
            *parts,
            first,
            b_in,
            second,
            *((stats,) if carry else ()),
            cost=pl.CostEstimate(
                flops=4 * size * width * hidden,
                bytes_accessed=4 * width * (hidden + size),
                transcendentals=size * hidden,
            ),
        )

    order = [(step, part) for part in range(PARTS) for step in far_steps]
    forwarded = {at: hop(visitors[at], "dp", 1) for at in order}
    answers = {}
    for at in order:
        theirs = run_expert([forwarded[at]], jnp.bfloat16, at[1] == 0)
        answers[at] = hop(theirs, "dp", 1)
    theirs = run_expert([beside], jnp.bfloat16)
    answer = hop(theirs, "dp", 1)
    owns = {}
    for step in far_steps:
        owns[step] = run_expert([visitors[step, part] for part in range(PARTS)], jnp.float32)
    returned = {}
    shared = answers[far_steps[0], 0]
    for step, part in order:
        carry = part == 0
        summed = kernel(
            functools.partial(far_kernel, part, carry),
            bf16(tall, full if carry else width),
            owns[step],
            answers[step, part],
            *((stats, shared) if carry else ()),
        )
        returned[step, part] = hop(summed, "dp", step)
    own = run_expert([home], jnp.float32)
    back, extra = [], None
    for part in range(PARTS):
        far = [returned[step, part] for step in far_steps]
        shapes = [bf16(CAP, full)] * each
        body = functools.partial(near_kernel, part, len(far))
        if part == 0:
            out = kernel(body, [bf16(CAP, LANES)] + shapes, own, answer, b_out, *far, stats, shared)
            extra, out = out[0], out[1:]
        else:
            out = kernel(body, shapes, own, answer, b_out, *far, extra)
        for place, slab in enumerate(out):
            k = part * each + place
            back.append(hop(slab, "expert", k) if k else slab)
    return tuple(
        kernel(
            functools.partial(combine_kernel, experts),
            [bf16(count, width), f32(2, 2)],
            target,
            gate,
            *back,
        )
    )


def solution(mesh):
    return jax.shard_map(
        on_device,
        mesh=mesh,
        in_specs=(
            P(AXES, None),
            P(),
            P(),
            P("expert", "dp", None),
            P("expert", "dp"),
            P("expert", "dp", None),
            P("expert", None),
            P(AXES),
            P(AXES),
            P(AXES),
        ),
        out_specs=(P(AXES, None), P()),
        check_vma=False,
    )
```

```python
import functools

import jax
import jax.numpy as jnp
from jax import lax
from jax.experimental import pallas as pl
from jax.experimental.pallas import tpu as pltpu
from jax.sharding import PartitionSpec as P

CAP = 16
PARTS = 2
LANES = 128
AXES = ("dp", "expert")
VMEM = pl.BlockSpec(memory_space=pltpu.VMEM)
PARAMS = pltpu.CompilerParams(vmem_limit_bytes=24 << 20)


def one_hot(rows, target):
    row = lax.broadcasted_iota(jnp.int32, (rows, target.shape[1]), 0)
    return (row == target).astype(jnp.float32).astype(jnp.bfloat16)


def spread_stats(total, rows, period):
    row = lax.broadcasted_iota(jnp.int32, (rows, LANES), 0) % period
    out = jnp.zeros((rows, LANES), jnp.float32)
    for piece in range(3):
        rounded = total.astype(jnp.bfloat16).astype(jnp.float32)
        out = jnp.where(row == piece, rounded, out)
        total = total - rounded
    return out.astype(jnp.bfloat16)


def join_stats(block):
    return jnp.sum(block.astype(jnp.float32), axis=0, keepdims=True)


def dispatch_kernel(tokens, gain, choice, slot, normed_out, target_out, buffer):
    values = tokens[...].astype(jnp.float32)
    center = values - jnp.mean(values, axis=-1, keepdims=True)
    spread = jnp.mean(center * center, axis=-1, keepdims=True)
    scaled = center * lax.rsqrt(spread + 1e-06) * gain[...].reshape(1, values.shape[1])
    normed = scaled.astype(jnp.bfloat16)
    normed_out[...] = normed
    kept = slot[...] >= 0
    relative = choice[...] ^ lax.axis_index("expert")
    target_out[...] = jnp.where(kept, relative * CAP + slot[...], -1)
    table = one_hot(buffer.shape[0], jnp.where(kept, choice[...] * CAP + slot[...], -1))
    buffer[...] = jnp.dot(table, normed, preferred_element_type=jnp.float32).astype(jnp.bfloat16)


def pack_kernel(received, *parts):
    me = lax.axis_index("expert")
    each = parts[0].shape[0] // CAP
    for k in range(received.shape[0] // CAP):
        slab = received[pl.ds(pl.multiple_of((me ^ k) * CAP, CAP), CAP)]
        at = (k % each) * CAP
        parts[k // each][at : at + CAP] = slab


def hold_kernel(w_in, w_out, first, second, sems):
    copies = []
    for source, target in ((w_in, first), (w_out, second)):
        size = target.shape[0] // 2
        for at in (0, size):
            rows = pl.ds(at, size)
            copies.append(pltpu.make_async_copy(source.at[rows], target.at[rows], sems.at[len(copies)]))
    for copy in copies:
        copy.start()
    for copy in copies:
        copy.wait()


def router_kernel(normed, router, choice, modality, gate_out, stats_out):
    logits = lax.dot_general(
        router[...], normed[...], (((1,), (1,)), ((), ())), preferred_element_type=jnp.float32
    )
    shifted = logits - jnp.max(logits, axis=0, keepdims=True)
    logp = shifted - jnp.log(jnp.sum(jnp.exp(shifted), axis=0, keepdims=True))
    probs = jnp.exp(logp)
    experts = probs.shape[0]
    expert = lax.broadcasted_iota(jnp.int32, probs.shape, 0)
    gate = jnp.sum(jnp.where(expert == choice[...], probs, 0.0), axis=0, keepdims=True)
    gate_out[...] = jnp.broadcast_to(gate, gate_out.shape)
    textual = (modality[...] == 1).astype(jnp.float32)
    entropy = -jnp.sum(probs * logp, axis=0, keepdims=True)
    lane = lax.broadcasted_iota(jnp.int32, (experts, LANES), 1)
    row = lax.broadcasted_iota(jnp.int32, (experts, LANES), 0)
    line = lane[0:1]
    stats = jnp.zeros((1, LANES), jnp.float32)
    for kind, select in enumerate((1.0 - textual, textual)):
        prob_sum = jnp.sum(probs * select, axis=1, keepdims=True)
        spread = jnp.where(lane == row + kind * experts, prob_sum, 0.0)
        stats = stats + jnp.sum(spread, axis=0, keepdims=True)
        ent_sum = jnp.sum(entropy * select, axis=1, keepdims=True)
        count = jnp.sum(select, axis=1, keepdims=True)
        stats = jnp.where(line == 2 * experts + kind, ent_sum, stats)
        stats = jnp.where(line == 2 * experts + 2 + kind, count, stats)
    stats_out[...] = jnp.broadcast_to(stats, stats_out.shape)


def expert_kernel(count, carry, *refs):
    parts, (first, first_bias, second), rest = refs[:count], refs[count : count + 3], refs[count + 3 :]
    out = rest[-1]
    rows = parts[0][...] if count == 1 else jnp.concatenate([part[...] for part in parts], axis=0)
    pre = lax.dot_general(
        rows, first[...], (((1,), (1,)), ((), ())), preferred_element_type=jnp.float32
    )
    pre = pre + first_bias[...].astype(jnp.float32)
    hidden = (0.5 * pre * (1.0 + lax.erf(pre * (0.5**0.5)))).astype(jnp.bfloat16)
    result = jnp.dot(hidden, second[...], preferred_element_type=jnp.float32)
    width = result.shape[1]
    out[:, :width] = result.astype(out.dtype)
    if carry:
        out[:, width:] = spread_stats(rest[0][0:1], out.shape[0], out.shape[0])


def far_kernel(index, carry, own, other, *refs):
    out = refs[-1]
    tall, width = out.shape[0], own.shape[1]
    mine = own[index * tall : (index + 1) * tall]
    out[:, :width] = (mine + other[:, :width].astype(jnp.float32)).astype(jnp.bfloat16)
    if carry:
        total = refs[0][0:1] + join_stats(refs[1][:, width:])
        out[:, width:] = spread_stats(total, tall, tall)


def near_kernel(index, far_count, own, other, bias, *refs):
    far, refs = refs[:far_count], refs[far_count:]
    tall, width = far[0].shape[0], own.shape[1]
    rows = slice(index * tall, (index + 1) * tall)
    result = own[rows] + other[rows].astype(jnp.float32) + bias[...].astype(jnp.float32)
    for block in far:
        result = result + block[:, :width].astype(jnp.float32)
    result = result.astype(jnp.bfloat16)
    if index == 0:
        stats, other_stats, extra_out = refs[:3]
        total = stats[0:1] + join_stats(other_stats[:, width:])
        for block in far:
            total = total + join_stats(block[:, width:])
        extra = spread_stats(total, CAP, CAP)
        extra_out[...] = extra
        slabs = refs[3:]
    else:
        extra = refs[0][...]
        slabs = refs[1:]
    for place, slab in enumerate(slabs):
        slab[:, :width] = result[place * CAP : (place + 1) * CAP]
        slab[:, width:] = extra


def combine_kernel(experts, target, gate, *refs):
    slabs, (out, aux) = refs[:-2], refs[-2:]
    width = out.shape[1]
    returned = jnp.concatenate([slab[...] for slab in slabs], axis=0)
    table = one_hot(returned.shape[0], target[...])
    fetched = lax.dot_general(
        table, returned[:, :width], (((0,), (0,)), ((), ())), preferred_element_type=jnp.float32
    )
    scale = jnp.transpose(gate[...])[:, 0:1]
    out[...] = (scale * fetched).astype(jnp.bfloat16)
    sums = join_stats(slabs[0][:, width:])
    have = {0: sums}
    for index in range(1, experts):
        have[index] = join_stats(slabs[index][:, width:])
    while len(have) > 1:
        have = {at // 2: have[at] + have[at + 1] for at in range(0, len(have), 2)}
    sums = have[0]
    lane = lax.broadcasted_iota(jnp.int32, sums.shape, 1)

    def pick(at):
        return jnp.sum(jnp.where(lane == at, sums, 0.0), axis=1, keepdims=True)

    row = lax.broadcasted_iota(jnp.int32, aux.shape, 0)
    column = lax.broadcasted_iota(jnp.int32, aux.shape, 1)
    result = jnp.zeros(aux.shape, jnp.float32)
    for kind in range(2):
        count = pick(2 * experts + 2 + kind)
        local = pick(2 * experts + kind) / count
        pbar = sums / count
        inside = (lane >= kind * experts) & (lane < (kind + 1) * experts)
        terms = jnp.where(inside, pbar * jnp.log(pbar), 0.0)
        spread = jnp.sum(terms, axis=1, keepdims=True)
        result = jnp.where((row == kind) & (column == 0), local, result)
        result = jnp.where((row == kind) & (column == 1), spread, result)
    aux[...] = result


def on_device(tokens, ln_gain, router, w_in, b_in, w_out, b_out, expert_choice, modality, slot):
    count, width = tokens.shape
    experts = router.shape[1]
    layers, senders = lax.axis_size("dp"), lax.axis_size("expert")
    assert w_in.shape[0] == 1 and experts == senders and layers % 4 == 0
    assert 2 * experts + 4 <= LANES and experts & (experts - 1) == 0
    hidden = w_in.shape[1]
    rows = experts * CAP
    tall = rows // PARTS
    full = width + LANES
    far_steps = [m ^ ((m >> 1) & 1) for m in range(2, layers, 2)]
    choice = expert_choice.reshape(1, count)
    normed, target, buffer = pl.pallas_call(
        dispatch_kernel,
        out_shape=[
            jax.ShapeDtypeStruct((count, width), jnp.bfloat16),
            jax.ShapeDtypeStruct((1, count), jnp.int32),
            jax.ShapeDtypeStruct((rows, width), jnp.bfloat16),
        ],
        in_specs=[VMEM] * 4,
        out_specs=[VMEM] * 3,
        name="dispatch",
    )(tokens, ln_gain, choice, slot.reshape(1, count))

    def kernel(body, shapes, *operands, cost=None, params=PARAMS):
        many = isinstance(shapes, list)
        return pl.pallas_call(
            body,
            out_shape=shapes,
            in_specs=[VMEM] * len(operands),
            out_specs=[VMEM] * len(shapes) if many else VMEM,
            cost_estimate=cost,
            compiler_params=params,
            name="kernel",
        )(*operands)

    def bf16(*shape):
        return jax.ShapeDtypeStruct(shape, jnp.bfloat16)

    def f32(*shape):
        return jax.ShapeDtypeStruct(shape, jnp.float32)

    def hop(block, axis, step):
        size = lax.axis_size(axis)
        return lax.ppermute(block, axis, [(i, i ^ step) for i in range(size)])

    each = experts // PARTS
    received = lax.all_to_all(
        buffer.reshape(experts, CAP, width), "expert", split_axis=0, concat_axis=0, tiled=True
    ).reshape(rows, width)
    homes = kernel(pack_kernel, [bf16(tall, width)] * PARTS, received)
    beside = [hop(homes[part], "dp", 1) for part in range(PARTS)]
    visitors = {
        (step, part): hop(homes[part], "dp", step)
        for part in range(PARTS)
        for step in far_steps
    }
    gate, stats = kernel(
        router_kernel,
        [f32(8, count), f32(8, LANES)],
        normed,
        router.T,
        choice,
        modality.reshape(1, count),
        params=None,
    )
    hold = pl.pallas_call(
        hold_kernel,
        out_shape=[pltpu.VMEM((hidden, width), jnp.bfloat16)] * 2,
        in_specs=[pl.BlockSpec(memory_space=pl.ANY)] * 2,
        out_specs=[VMEM] * 2,
        scratch_shapes=[pltpu.SemaphoreType.DMA((4,))],
        compiler_params=pltpu.CompilerParams(vmem_limit_bytes=56 << 20),
        name="kernel",
    )
    first, second = hold(w_in.reshape(hidden, width), w_out.reshape(hidden, width))
    first = pltpu.with_memory_space_constraint(first, pltpu.VMEM)
    second = pltpu.with_memory_space_constraint(second, pltpu.VMEM)

    def run_expert(parts, dtype, carry=False):
        size = sum(part.shape[0] for part in parts)
        return kernel(
            functools.partial(expert_kernel, len(parts), carry),
            jax.ShapeDtypeStruct((size, full if carry else width), dtype),
            *parts,
            first,
            b_in,
            second,
            *((stats,) if carry else ()),
            cost=pl.CostEstimate(
                flops=4 * size * width * hidden,
                bytes_accessed=4 * width * (hidden + size),
                transcendentals=size * hidden,
            ),
        )

    order = [(step, part) for part in range(PARTS) for step in far_steps]
    forwarded = {at: hop(visitors[at], "dp", 1) for at in order}
    answers = {}
    for at in order:
        theirs = run_expert([forwarded[at]], jnp.bfloat16, at[1] == 0)
        answers[at] = hop(theirs, "dp", 1)
    theirs = run_expert(beside, jnp.bfloat16)
    answer = hop(theirs, "dp", 1)
    owns = {}
    for step in far_steps:
        owns[step] = run_expert([visitors[step, part] for part in range(PARTS)], jnp.float32)
    returned = {}
    shared = answers[far_steps[0], 0]
    for step, part in order:
        carry = part == 0
        summed = kernel(
            functools.partial(far_kernel, part, carry),
            bf16(tall, full if carry else width),
            owns[step],
            answers[step, part],
            *((stats, shared) if carry else ()),
        )
        returned[step, part] = hop(summed, "dp", step)
    own = run_expert(homes, jnp.float32)
    back, extra = [], None
    for part in range(PARTS):
        far = [returned[step, part] for step in far_steps]
        shapes = [bf16(CAP, full)] * each
        body = functools.partial(near_kernel, part, len(far))
        if part == 0:
            out = kernel(body, [bf16(CAP, LANES)] + shapes, own, answer, b_out, *far, stats, shared)
            extra, out = out[0], out[1:]
        else:
            out = kernel(body, shapes, own, answer, b_out, *far, extra)
        for place, slab in enumerate(out):
            k = part * each + place
            back.append(hop(slab, "expert", k) if k else slab)
    return tuple(
        kernel(
            functools.partial(combine_kernel, experts),
            [bf16(count, width), f32(2, 2)],
            target,
            gate,
            *back,
        )
    )


def solution(mesh):
    return jax.shard_map(
        on_device,
        mesh=mesh,
        in_specs=(
            P(AXES, None),
            P(),
            P(),
            P("expert", "dp", None),
            P("expert", "dp"),
            P("expert", "dp", None),
            P("expert", None),
            P(AXES),
            P(AXES),
            P(AXES),
        ),
        out_specs=(P(AXES, None), P()),
        check_vma=False,
    )
```

```python
import functools

import jax
import jax.numpy as jnp
from jax import lax
from jax.experimental import pallas as pl
from jax.experimental.pallas import tpu as pltpu
from jax.sharding import PartitionSpec as P

CAP = 16
PARTS = 2
LANES = 128
AXES = ("dp", "expert")
VMEM = pl.BlockSpec(memory_space=pltpu.VMEM)
PARAMS = pltpu.CompilerParams(vmem_limit_bytes=24 << 20)


def one_hot(rows, target):
    row = lax.broadcasted_iota(jnp.int32, (rows, target.shape[1]), 0)
    return (row == target).astype(jnp.float32).astype(jnp.bfloat16)


def spread_stats(total, rows, period):
    row = lax.broadcasted_iota(jnp.int32, (rows, LANES), 0) % period
    out = jnp.zeros((rows, LANES), jnp.float32)
    for piece in range(3):
        rounded = total.astype(jnp.bfloat16).astype(jnp.float32)
        out = jnp.where(row == piece, rounded, out)
        total = total - rounded
    return out.astype(jnp.bfloat16)


def join_stats(block):
    return jnp.sum(block.astype(jnp.float32), axis=0, keepdims=True)


def dispatch_kernel(tokens, gain, choice, slot, normed_out, target_out, odds, *evens):
    values = tokens[...].astype(jnp.float32)
    center = values - jnp.mean(values, axis=-1, keepdims=True)
    spread = jnp.mean(center * center, axis=-1, keepdims=True)
    scaled = center * lax.rsqrt(spread + 1e-06) * gain[...].reshape(1, values.shape[1])
    normed = scaled.astype(jnp.bfloat16)
    normed_out[...] = normed
    relative = choice[...] ^ lax.axis_index("expert")
    target = jnp.where(slot[...] >= 0, relative * CAP + slot[...], -1)
    target_out[...] = target
    rows = odds.shape[0] + len(evens) * CAP
    table = one_hot(rows, target)
    packed = jnp.dot(table, normed, preferred_element_type=jnp.float32).astype(jnp.bfloat16)
    for index, even in enumerate(evens):
        start = 2 * index * CAP
        even[...] = packed[start : start + CAP]
        odds[index * CAP : (index + 1) * CAP] = packed[start + CAP : start + 2 * CAP]


def join_kernel(first, *refs):
    count = len(refs) // 2
    partner, evens, outs = refs[0], refs[1 : count + 1], refs[count + 1 :]
    for index in range(count):
        start = (first + index) * CAP
        outs[index][:CAP] = evens[index][...]
        outs[index][CAP:] = partner[start : start + CAP]


def pack_kernel(opening, *refs):
    blocks, out = list(refs[:-1]), refs[-1]
    at = 0
    for index, block in enumerate(blocks):
        size = CAP if opening and index == 1 else block.shape[0]
        out[at : at + size] = block[:size]
        at += size


def hold_kernel(w_in, w_out, first, second, sems):
    copies = []
    for source, target in ((w_in, first), (w_out, second)):
        size = target.shape[0] // 2
        for at in (0, size):
            rows = pl.ds(at, size)
            copies.append(pltpu.make_async_copy(source.at[rows], target.at[rows], sems.at[len(copies)]))
    for copy in copies:
        copy.start()
    for copy in copies:
        copy.wait()


def router_kernel(normed, router, choice, modality, gate_out, stats_out):
    logits = lax.dot_general(
        router[...], normed[...], (((1,), (1,)), ((), ())), preferred_element_type=jnp.float32
    )
    shifted = logits - jnp.max(logits, axis=0, keepdims=True)
    logp = shifted - jnp.log(jnp.sum(jnp.exp(shifted), axis=0, keepdims=True))
    probs = jnp.exp(logp)
    experts = probs.shape[0]
    expert = lax.broadcasted_iota(jnp.int32, probs.shape, 0)
    gate = jnp.sum(jnp.where(expert == choice[...], probs, 0.0), axis=0, keepdims=True)
    gate_out[...] = jnp.broadcast_to(gate, gate_out.shape)
    textual = (modality[...] == 1).astype(jnp.float32)
    entropy = -jnp.sum(probs * logp, axis=0, keepdims=True)
    lane = lax.broadcasted_iota(jnp.int32, (experts, LANES), 1)
    row = lax.broadcasted_iota(jnp.int32, (experts, LANES), 0)
    line = lane[0:1]
    stats = jnp.zeros((1, LANES), jnp.float32)
    for kind, select in enumerate((1.0 - textual, textual)):
        prob_sum = jnp.sum(probs * select, axis=1, keepdims=True)
        spread = jnp.where(lane == row + kind * experts, prob_sum, 0.0)
        stats = stats + jnp.sum(spread, axis=0, keepdims=True)
        ent_sum = jnp.sum(entropy * select, axis=1, keepdims=True)
        count = jnp.sum(select, axis=1, keepdims=True)
        stats = jnp.where(line == 2 * experts + kind, ent_sum, stats)
        stats = jnp.where(line == 2 * experts + 2 + kind, count, stats)
    stats_out[...] = jnp.broadcast_to(stats, stats_out.shape)


def expert_kernel(count, carry, *refs):
    parts, (first, first_bias, second), rest = refs[:count], refs[count : count + 3], refs[count + 3 :]
    out = rest[-1]
    rows = parts[0][...] if count == 1 else jnp.concatenate([part[...] for part in parts], axis=0)
    pre = lax.dot_general(
        rows, first[...], (((1,), (1,)), ((), ())), preferred_element_type=jnp.float32
    )
    pre = pre + first_bias[...].astype(jnp.float32)
    hidden = (0.5 * pre * (1.0 + lax.erf(pre * (0.5**0.5)))).astype(jnp.bfloat16)
    result = jnp.dot(hidden, second[...], preferred_element_type=jnp.float32)
    width = result.shape[1]
    out[:, :width] = result.astype(out.dtype)
    if carry:
        out[:, width:] = spread_stats(rest[0][0:1], out.shape[0], out.shape[0])


def far_kernel(index, carry, own, other, *refs):
    out = refs[-1]
    tall, width = out.shape[0], own.shape[1]
    mine = own[index * tall : (index + 1) * tall]
    out[:, :width] = (mine + other[:, :width].astype(jnp.float32)).astype(jnp.bfloat16)
    if carry:
        total = refs[0][0:1] + join_stats(refs[1][:, width:])
        out[:, width:] = spread_stats(total, tall, tall)


def near_kernel(index, far_count, own, other, bias, *refs):
    far, refs = refs[:far_count], refs[far_count:]
    tall, width = far[0].shape[0], own.shape[1]
    rows = slice(index * tall, (index + 1) * tall)
    result = own[rows] + other[rows].astype(jnp.float32) + bias[...].astype(jnp.float32)
    for block in far:
        result = result + block[:, :width].astype(jnp.float32)
    result = result.astype(jnp.bfloat16)
    if index == 0:
        stats, other_stats, extra_out = refs[:3]
        total = stats[0:1] + join_stats(other_stats[:, width:])
        for block in far:
            total = total + join_stats(block[:, width:])
        extra = spread_stats(total, CAP, CAP)
        extra_out[...] = extra
        slabs = refs[3:]
    else:
        extra = refs[0][...]
        slabs = refs[1:]
    odds, evens = slabs[0], slabs[1:]
    for place, even in enumerate(evens):
        start = 2 * place * CAP
        even[:, :width] = result[start : start + CAP]
        even[:, width:] = extra
        here = slice(place * CAP, (place + 1) * CAP)
        odds[here, :width] = result[start + CAP : start + 2 * CAP]
        odds[here, width:] = extra


def combine_kernel(experts, target, gate, *refs):
    slabs, (out, aux) = refs[:-2], refs[-2:]
    width = out.shape[1]
    blocks = [slabs[0][...], slabs[1][:CAP]] + [slab[...] for slab in slabs[2:]]
    returned = jnp.concatenate(blocks, axis=0)
    table = one_hot(returned.shape[0], target[...])
    fetched = lax.dot_general(
        table, returned[:, :width], (((0,), (0,)), ((), ())), preferred_element_type=jnp.float32
    )
    scale = jnp.transpose(gate[...])[:, 0:1]
    out[...] = (scale * fetched).astype(jnp.bfloat16)
    have = {k: join_stats(returned[k * CAP : (k + 1) * CAP, width:]) for k in range(experts)}
    while len(have) > 1:
        have = {at // 2: have[at] + have[at + 1] for at in range(0, len(have), 2)}
    sums = have[0]
    lane = lax.broadcasted_iota(jnp.int32, sums.shape, 1)

    def pick(at):
        return jnp.sum(jnp.where(lane == at, sums, 0.0), axis=1, keepdims=True)

    row = lax.broadcasted_iota(jnp.int32, aux.shape, 0)
    column = lax.broadcasted_iota(jnp.int32, aux.shape, 1)
    result = jnp.zeros(aux.shape, jnp.float32)
    for kind in range(2):
        count = pick(2 * experts + 2 + kind)
        local = pick(2 * experts + kind) / count
        pbar = sums / count
        inside = (lane >= kind * experts) & (lane < (kind + 1) * experts)
        terms = jnp.where(inside, pbar * jnp.log(pbar), 0.0)
        spread = jnp.sum(terms, axis=1, keepdims=True)
        result = jnp.where((row == kind) & (column == 0), local, result)
        result = jnp.where((row == kind) & (column == 1), spread, result)
    aux[...] = result


def on_device(tokens, ln_gain, router, w_in, b_in, w_out, b_out, expert_choice, modality, slot):
    count, width = tokens.shape
    experts = router.shape[1]
    layers, senders = lax.axis_size("dp"), lax.axis_size("expert")
    assert w_in.shape[0] == 1 and experts == senders and layers % 4 == 0
    assert 2 * experts + 4 <= LANES and experts & (experts - 1) == 0
    hidden = w_in.shape[1]
    rows = experts * CAP
    tall = rows // PARTS
    full = width + LANES
    far_steps = [m ^ ((m >> 1) & 1) for m in range(2, layers, 2)]
    choice = expert_choice.reshape(1, count)
    pairs = experts // 2
    normed, target, odds, *evens = pl.pallas_call(
        dispatch_kernel,
        out_shape=[
            jax.ShapeDtypeStruct((count, width), jnp.bfloat16),
            jax.ShapeDtypeStruct((1, count), jnp.int32),
            pltpu.VMEM((pairs * CAP, width), jnp.bfloat16),
        ]
        + [pltpu.VMEM((CAP, width), jnp.bfloat16)] * pairs,
        in_specs=[VMEM] * 4,
        out_specs=[VMEM] * (3 + pairs),
        name="dispatch",
    )(tokens, ln_gain, choice, slot.reshape(1, count))

    def kernel(body, shapes, *operands, cost=None, params=PARAMS):
        many = isinstance(shapes, list)
        return pl.pallas_call(
            body,
            out_shape=shapes,
            in_specs=[VMEM] * len(operands),
            out_specs=[VMEM] * len(shapes) if many else VMEM,
            cost_estimate=cost,
            compiler_params=params,
            name="kernel",
        )(*operands)

    def bf16(*shape):
        return jax.ShapeDtypeStruct(shape, jnp.bfloat16)

    def f32(*shape):
        return jax.ShapeDtypeStruct(shape, jnp.float32)

    def hop(block, axis, step):
        size = lax.axis_size(axis)
        return lax.ppermute(block, axis, [(i, i ^ step) for i in range(size)])

    partner = hop(odds, "expert", 1)
    joined = kernel(
        functools.partial(join_kernel, 1), [bf16(2 * CAP, width)] * (pairs - 1), partner, *evens[1:]
    )
    came = [hop(block, "expert", 2 * j + 2) for j, block in enumerate(joined)]
    share = pairs // PARTS
    homes = []
    for part in range(PARTS):
        blocks = came[max(part * share - 1, 0) : (part + 1) * share - 1]
        if part == 0:
            blocks = [evens[0], partner] + blocks
        homes.append(kernel(functools.partial(pack_kernel, part == 0), bf16(tall, width), *blocks))
    beside = [hop(homes[part], "dp", 1) for part in range(PARTS)]
    visitors = {
        (step, part): hop(homes[part], "dp", step)
        for part in range(PARTS)
        for step in far_steps
    }
    gate, stats = kernel(
        router_kernel,
        [f32(8, count), f32(8, LANES)],
        normed,
        router.T,
        choice,
        modality.reshape(1, count),
        params=None,
    )
    hold = pl.pallas_call(
        hold_kernel,
        out_shape=[pltpu.VMEM((hidden, width), jnp.bfloat16)] * 2,
        in_specs=[pl.BlockSpec(memory_space=pl.ANY)] * 2,
        out_specs=[VMEM] * 2,
        scratch_shapes=[pltpu.SemaphoreType.DMA((4,))],
        compiler_params=pltpu.CompilerParams(vmem_limit_bytes=56 << 20),
        name="kernel",
    )
    first, second = hold(w_in.reshape(hidden, width), w_out.reshape(hidden, width))
    first = pltpu.with_memory_space_constraint(first, pltpu.VMEM)
    second = pltpu.with_memory_space_constraint(second, pltpu.VMEM)

    def run_expert(parts, dtype, carry=False):
        size = sum(part.shape[0] for part in parts)
        return kernel(
            functools.partial(expert_kernel, len(parts), carry),
            jax.ShapeDtypeStruct((size, full if carry else width), dtype),
            *parts,
            first,
            b_in,
            second,
            *((stats,) if carry else ()),
            cost=pl.CostEstimate(
                flops=4 * size * width * hidden,
                bytes_accessed=4 * width * (hidden + size),
                transcendentals=size * hidden,
            ),
        )

    order = [(step, part) for part in range(PARTS) for step in far_steps]
    forwarded = {at: hop(visitors[at], "dp", 1) for at in order}
    answers = {}
    for at in order:
        theirs = run_expert([forwarded[at]], jnp.bfloat16, at[1] == 0)
        answers[at] = hop(theirs, "dp", 1)
    theirs = run_expert(beside, jnp.bfloat16)
    answer = hop(theirs, "dp", 1)
    owns = {}
    for step in far_steps:
        owns[step] = run_expert([visitors[step, part] for part in range(PARTS)], jnp.float32)
    returned = {}
    shared = answers[far_steps[0], 0]
    for step, part in order:
        carry = part == 0
        summed = kernel(
            functools.partial(far_kernel, part, carry),
            bf16(tall, full if carry else width),
            owns[step],
            answers[step, part],
            *((stats, shared) if carry else ()),
        )
        returned[step, part] = hop(summed, "dp", step)
    own = run_expert(homes, jnp.float32)
    back, extra = [], None
    for part in range(PARTS):
        far = [returned[step, part] for step in far_steps]
        shapes = [bf16(share * CAP, full)] + [bf16(CAP, full)] * share
        body = functools.partial(near_kernel, part, len(far))
        if part == 0:
            extra, odds, *evens = kernel(
                body, [bf16(CAP, LANES)] + shapes, own, answer, b_out, *far, stats, shared
            )
        else:
            odds, *evens = kernel(body, shapes, own, answer, b_out, *far, extra)
        partner = hop(odds, "expert", 1)
        lead = 1 if part == 0 else 0
        if part == 0:
            back += [evens[0], partner]
        if share > lead:
            joined = kernel(
                functools.partial(join_kernel, lead),
                [bf16(2 * CAP, full)] * (share - lead),
                partner,
                *evens[lead:],
            )
            for index, block in enumerate(joined):
                k = 2 * (part * share + lead + index)
                back.append(hop(block, "expert", k))
    return tuple(
        kernel(
            functools.partial(combine_kernel, experts),
            [bf16(count, width), f32(2, 2)],
            target,
            gate,
            *back,
        )
    )


def solution(mesh):
    return jax.shard_map(
        on_device,
        mesh=mesh,
        in_specs=(
            P(AXES, None),
            P(),
            P(),
            P("expert", "dp", None),
            P("expert", "dp"),
            P("expert", "dp", None),
            P("expert", None),
            P(AXES),
            P(AXES),
            P(AXES),
        ),
        out_specs=(P(AXES, None), P()),
        check_vma=False,
    )
```
